32 devices in a mesh: blocks: 2 (over y), sec: 8 (over z, x), pln: 2 (over core).
Axes of the slice: x: 2, y: 2, z: 4, core: 2. Of those that a mesh axis runs over, the one named last changes fastest.
Arguments:
- section_tiles: float32 [16, 256, 512], P(('blocks', 'sec'), 'pln'), parts along dimension 0, may hold values from -6 to 6
Outputs:
- flow_scores: float32 [16, 4, 8, 4096], P(('blocks', 'sec'), 'pln'), parts along dimension 0
The draws below stay inside these ranges and needn't reach their ends.
There are 2 independent parts, one for each index of `blocks`. The reference program is written for one: setup_inputs(seed, part) draws one part's arguments, and reference() takes and returns one part's arrays. A program takes and returns all parts, laid end to end along the dimension named above; each array names one. Nothing has to cross between parts.
All inputs are finite; a program needn't handle non-finite values.
Results may differ from the reference program's by a relative error of at most 0.0003.
Values sent between devices are 32-bit elements; how exact they have to be, the bound alone decides.
A program may use at most 64 MiB of HBM per device.

```python
import jax
import jax.numpy as jnp
from jax import lax

COLS = 512
PATCH = 128
STRIDE = 64
CROP = 64
MARGIN = 32
NSEC = 8
HEIGHT = 256


def levels(own_key, shape, shards, smallest, high):
    gain, own = 1.0, jax.random.fold_in(own_key, 6)
    for dim, shards_of in shards:
        heights = jnp.exp(jax.random.uniform(jax.random.fold_in(own, dim), (shards_of,), jnp.float32, smallest / len(shards), high / len(shards)))
        gain = gain * jnp.repeat(heights, shape[dim] // shards_of).reshape([-1 if axis == dim else 1 for axis in range(len(shape))])
    return gain


def bell_draw(key, shape, spread, reach, split=(), kind=jnp.bfloat16):
    drawn = spread * jax.random.normal(key, shape, jnp.float32)
    if split:
        drawn = drawn * levels(key, shape, split, -0.22, 0.18)
    return jnp.clip(drawn, -reach, reach).astype(kind)


def setup_inputs(seed: int = 0, part: int = 0) -> dict:
    arg_keys = jax.random.split(jax.random.key(seed), 2)
    part_splits = jax.random.split(jax.random.fold_in(arg_keys[1], part), 2)
    return {
        "section_tiles": bell_draw(part_splits[0], (NSEC, HEIGHT, COLS), 1.0, 6.0, ((0, 8), (1, 2)), jnp.float32),
    }


def patch_stack(section_image):
    padded = jnp.pad(section_image, ((MARGIN, MARGIN), (MARGIN, MARGIN)))
    grid_rows = section_image.shape[0] // STRIDE
    grid_cols = section_image.shape[1] // STRIDE
    blocks = padded.reshape(grid_rows + 1, STRIDE, grid_cols + 1, STRIDE)
    blocks = blocks.transpose(0, 2, 1, 3)
    upper_half = jnp.concatenate([blocks[:-1, :-1], blocks[:-1, 1:]], axis=3)
    lower_half = jnp.concatenate([blocks[1:, :-1], blocks[1:, 1:]], axis=3)
    return jnp.concatenate([upper_half, lower_half], axis=2)


def section_scores(section_tiles, section_index):
    def spectrum(distance):
        source = jnp.maximum(section_index - distance, 0).astype(jnp.int32)
        picked = lax.dynamic_index_in_dim(section_tiles, source, 0, keepdims=False)
        present = section_index >= distance
        picked = jnp.where(present, picked, jnp.zeros_like(picked))
        return jnp.fft.fft2(patch_stack(picked))

    own_spec = spectrum(0)
    crop_start = PATCH // 2 - CROP // 2
    surfaces = []
    for distance in (1, 2):
        earlier_spec = spectrum(distance)
        circular = jnp.fft.ifft2(own_spec * jnp.conj(earlier_spec)).real
        circular = jnp.fft.fftshift(circular, axes=(2, 3))
        cropped = circular[:, :, crop_start:crop_start + CROP, crop_start:crop_start + CROP] / PATCH
        surfaces.append(cropped)
    consensus = surfaces[0] + surfaces[1] + surfaces[0] * surfaces[1]
    return consensus.reshape(consensus.shape[0], consensus.shape[1], CROP * CROP)


def reference(section_tiles):
    indices = jnp.arange(section_tiles.shape[0], dtype=jnp.int32)
    consensus = lax.map(lambda section_index: section_scores(section_tiles, section_index), indices)
    padded = jnp.pad(consensus, ((0, 0), (1, 1), (1, 1), (0, 0)))
    rows_mix = padded[:, :-2] + 2.0 * padded[:, 1:-1] + padded[:, 2:]
    mixed = rows_mix[:, :, :-2] + 2.0 * rows_mix[:, :, 1:-1] + rows_mix[:, :, 2:]
    return mixed / 16.0
```

```python
import functools
import math

import jax
import jax.numpy as jnp
import numpy as np
from jax import lax
from jax.experimental import pallas as pl
from jax.experimental.pallas import tpu as pltpu
from jax.sharding import PartitionSpec as P

PATCH = 128
STRIDE = 64
CROP = 64
MARGIN = 32
HALF = 72
TILE = 128
MESH = pl.DeviceIdType.MESH


def split_table(table):
    high = np.asarray(table, np.float32).astype(jnp.bfloat16)
    low = (np.asarray(table, np.float32) - high.astype(np.float32)).astype(jnp.bfloat16)
    return high, low


def angles(left, right):
    return np.mod(np.outer(left, right), PATCH) * (2.0 * math.pi / PATCH)


def tables():
    spots = np.arange(PATCH)
    freqs = np.arange(PATCH // 2 + 1)
    lags = np.arange(CROP) - CROP // 2
    rows = np.zeros((2 * HALF, PATCH))
    rows[: len(freqs)] = np.cos(angles(freqs, spots))
    rows[HALF : HALF + len(freqs)] = -np.sin(angles(freqs, spots))
    rows_hi, rows_lo = split_table(rows)
    row_table = np.concatenate([rows_hi, rows_hi, rows_lo], axis=1)
    cos, sin = np.cos(angles(spots, spots)), np.sin(angles(spots, spots))
    cols_hi, cols_lo = split_table(np.block([[cos, -sin], [sin, cos]]))
    cos, sin = np.cos(angles(spots, lags)), np.sin(angles(spots, lags))
    none = np.zeros_like(cos)
    lag_hi, lag_lo = split_table(
        np.block(
            [
                [cos, none, sin, none],
                [-sin, none, cos, none],
                [none, cos, none, sin],
                [none, -sin, none, cos],
            ]
        )
    )
    order = np.concatenate([lags[0::2], lags[1::2]])
    weight = np.where((freqs == 0) | (freqs == PATCH // 2), 1.0, 2.0) / PATCH**3
    ups = np.zeros((CROP, 2 * HALF))
    ups[:, : len(freqs)] = np.cos(angles(order, freqs)) * weight
    ups[:, HALF : HALF + len(freqs)] = -np.sin(angles(order, freqs)) * weight
    ups_hi, ups_lo = split_table(ups)
    up_table = np.concatenate([ups_hi, ups_hi, ups_lo], axis=1)
    return row_table, cols_hi, cols_lo, lag_hi, lag_lo, up_table


def halves(value):
    high = value.astype(jnp.bfloat16)
    return high, (value - high.astype(jnp.float32)).astype(jnp.bfloat16)


def dot(left, right):
    return jnp.dot(left, right, preferred_element_type=jnp.float32)


def kernel(
    n_sec, x_hbm, row_hbm, chi_hbm, clo_hbm, lhi_hbm, llo_hbm, up_hbm, o_ref,
    field, row_t, chi_t, clo_t, lhi_t, llo_t, up_t, spec, mixed, rim,
    load_sem, halo_sem, one_send, two_send, relay_send, one_recv, two_recv,
    fwd_one_send, fwd_two_send, fwd_one_recv, fwd_two_recv, rim_sem,
):
    rows, cols = x_hbm.shape
    tiles = cols // TILE
    patch_rows, grid_cols = rows // STRIDE, cols // STRIDE
    s, p = lax.axis_index("sec"), lax.axis_index("pln")
    other = 1 - p
    odd = lax.rem(s, 2) == 1
    has_one, has_two = s >= 1, s >= 2
    edge = other * (rows - MARGIN)
    far = p * (rows + MARGIN)

    loads = [
        pltpu.make_async_copy(src, dst, load_sem.at[n])
        for n, (src, dst) in enumerate(
            [
                (x_hbm, field.at[0, pl.ds(MARGIN, rows), :]),
                (row_hbm, row_t), (chi_hbm, chi_t), (clo_hbm, clo_t),
                (lhi_hbm, lhi_t), (llo_hbm, llo_t), (up_hbm, up_t),
            ]
        )
    ]
    for load in loads:
        load.start()

    barrier = pltpu.get_barrier_semaphore()
    count = jnp.int32(1)
    pl.semaphore_signal(barrier, inc=1, device_id={"pln": other}, device_id_type=MESH)
    for step in (-2, -1, 1, 2):
        there = jnp.logical_and(s + step >= 0, s + step < n_sec)
        count = count + there.astype(jnp.int32)

        @pl.when(there)
        def _(step=step):
            pl.semaphore_signal(barrier, inc=1, device_id={"sec": s + step}, device_id_type=MESH)

    pl.semaphore_wait(barrier, count)

    def remote(src, dst, send, recv, where):
        return pltpu.make_async_remote_copy(
            src_ref=src, dst_ref=dst, send_sem=send, recv_sem=recv,
            device_id=where, device_id_type=MESH,
        )

    def wrapped(step):
        return {"sec": lax.rem(s + step + n_sec, n_sec)}

    def main(d, t):
        return field.at[d, pl.ds(MARGIN, rows), pl.ds(t * TILE, TILE)]

    def source(t):
        return x_hbm.at[:, pl.ds(t * TILE, TILE)]

    def direct_one(t):
        return remote(source(t), main(1, t), one_send.at[t], one_recv.at[t], wrapped(1))

    def direct_two(t):
        return remote(source(t), main(2, t), two_send.at[t], two_recv.at[t], wrapped(2))

    def relay(t):
        return remote(main(2, t), main(1, t), relay_send.at[t], one_recv.at[t], wrapped(-1))

    def forward(d, t):
        send, recv = ((fwd_one_send, fwd_one_recv), (fwd_two_send, fwd_two_recv))[d - 1]
        lanes = pl.ds(t * TILE, TILE)
        return remote(
            field.at[d, pl.ds(pl.multiple_of(MARGIN + edge, MARGIN), MARGIN), lanes],
            field.at[d, pl.ds(pl.multiple_of(far, MARGIN), MARGIN), lanes],
            send.at[t], recv.at[t], {"pln": other},
        )

    halo = remote(
        x_hbm.at[pl.ds(pl.multiple_of(edge, MARGIN), MARGIN), :],
        field.at[0, pl.ds(pl.multiple_of(far, MARGIN), MARGIN), :],
        halo_sem.at[0], halo_sem.at[1], {"pln": other},
    )
    gives_one = jnp.logical_and(jnp.logical_not(odd), s + 1 < n_sec)
    gives_two = s + 2 < n_sec
    relays = jnp.logical_and(odd, s >= 3)

    halo.start()

    @pl.when(gives_two)
    def _():
        for t in range(tiles):
            direct_two(t).start()

    @pl.when(gives_one)
    def _():
        for t in range(tiles):
            direct_one(t).start()

    blank = pl.ds(pl.multiple_of(far, MARGIN), MARGIN)
    for d in range(3):
        field[d, blank, :] = jnp.zeros((MARGIN, cols), jnp.float32)
    for d, here in ((1, has_one), (2, has_two)):

        @pl.when(jnp.logical_not(here))
        def _(d=d):
            field[d] = jnp.zeros(field.shape[1:], jnp.float32)

    lane = lax.broadcasted_iota(jnp.int32, (2 * HALF, TILE), 1)

    def spectrum(d, i):
        slab = field[d, pl.ds(pl.multiple_of(i * STRIDE, STRIDE), PATCH), :]
        high, low = halves(slab)
        strips = dot(row_t[...], jnp.concatenate([high, low, high], axis=0))
        zero = jnp.zeros((2 * HALF, TILE), jnp.float32)
        parts = [zero] + [strips[:, t * TILE : (t + 1) * TILE] for t in range(tiles)] + [zero]
        stack = []
        for t in range(1, tiles + 1):
            for picked in (
                jnp.where(lane < PATCH - MARGIN, parts[t], parts[t - 1]),
                jnp.where(lane >= MARGIN, parts[t], parts[t + 1]),
            ):
                stack.append(jnp.concatenate([picked[:HALF], picked[HALF:]], axis=1))
        high, low = halves(jnp.concatenate(stack, axis=0))
        return dot(high, chi_t[...]) + dot(low, chi_t[...]) + dot(high, clo_t[...])

    for load in loads:
        load.wait()
    halo.wait_recv()
    for i in range(patch_rows):
        spec[i] = spectrum(0, i)

    for t in range(tiles):

        @pl.when(has_two)
        def _(t=t):
            direct_two(t).wait_recv()

            @pl.when(relays)
            def _():
                relay(t).start()

            forward(2, t).start()

        @pl.when(has_one)
        def _(t=t):
            direct_one(t).wait_recv()
            forward(1, t).start()

    @pl.when(has_one)
    def _():
        for t in range(tiles):
            forward(1, t).wait_recv()

    @pl.when(has_two)
    def _():
        for t in range(tiles):
            forward(2, t).wait_recv()

    def cross(own, back):
        own_re, own_im = own[:, :PATCH], own[:, PATCH:]
        back_re, back_im = back[:, :PATCH], back[:, PATCH:]
        return [own_re * back_re + own_im * back_im, own_im * back_re - own_re * back_im]

    left = lax.broadcasted_iota(jnp.int32, (CROP // 2, TILE), 1) < CROP

    def patch_row(i):
        own = spec[i]
        both = jnp.concatenate(cross(own, spectrum(1, i)) + cross(own, spectrum(2, i)), axis=1)
        high, low = halves(both)
        half = dot(high, lhi_t[...]) + dot(low, lhi_t[...]) + dot(high, llo_t[...])
        columns = [
            jnp.concatenate([half[j * HALF : (j + 1) * HALF, :TILE], half[j * HALF : (j + 1) * HALF, TILE:]], axis=0)
            for j in range(grid_cols)
        ]
        high, low = halves(jnp.concatenate(columns, axis=1))
        surfaces = dot(up_t[...], jnp.concatenate([high, low, high], axis=0))
        joined = [jnp.zeros((CROP // 2, TILE), jnp.float32)]
        for j in range(grid_cols):
            here = surfaces[:, j * TILE : (j + 1) * TILE]
            there = pltpu.roll(here, CROP, 1)
            agreed = here + there + here * there
            joined.append(jnp.where(left, agreed[: CROP // 2], agreed[CROP // 2 :]))
        joined.append(joined[0])
        for j in range(grid_cols):
            mixed[i, j] = joined[j] + 2.0 * joined[j + 1] + joined[j + 2]

    rim_row = (patch_rows - 1) * other
    send_rim = remote(mixed.at[rim_row], rim, rim_sem.at[0], rim_sem.at[1], {"pln": other})
    patch_row(rim_row)
    send_rim.start()
    for step in range(1, patch_rows):
        patch_row(step * p + (patch_rows - 1 - step) * other)

    send_rim.wait_recv()
    above = (p == 1).astype(jnp.float32)
    below = (p == 0).astype(jnp.float32)
    for i in range(patch_rows):
        for j in range(grid_cols):
            up = mixed[i - 1, j] if i > 0 else rim[j] * above
            down = mixed[i + 1, j] if i < patch_rows - 1 else rim[j] * below
            o_ref[i, pl.ds(j, CROP // 2, stride=grid_cols), :] = (
                up + 2.0 * mixed[i, j] + down
            ) * (1.0 / 16.0)

    halo.wait_send()
    send_rim.wait_send()
    for held, copy in (
        (gives_two, direct_two), (gives_one, direct_one), (relays, relay),
        (has_one, functools.partial(forward, 1)), (has_two, functools.partial(forward, 2)),
    ):

        @pl.when(held)
        def _(copy=copy):
            for t in range(tiles):
                copy(t).wait_send()


def body(section_tiles):
    tile = section_tiles[0]
    rows, cols = tile.shape
    n_sec, n_pln = lax.axis_size("sec"), lax.axis_size("pln")
    assert n_pln == 2 and n_sec % 2 == 0 and cols % TILE == 0
    patch_rows, grid_cols, tiles = rows // STRIDE, cols // STRIDE, cols // TILE
    consts = tables()
    dma = pltpu.SemaphoreType.DMA
    out = pl.pallas_call(
        functools.partial(kernel, n_sec),
        out_shape=jax.ShapeDtypeStruct((patch_rows, CROP // 2 * grid_cols, TILE), jnp.float32),
        in_specs=[pl.BlockSpec(memory_space=pl.ANY)] * (1 + len(consts)),
        out_specs=pl.BlockSpec(memory_space=pltpu.VMEM),
        scratch_shapes=[
            pltpu.VMEM((3, rows + 2 * MARGIN, cols), jnp.float32),
            *[pltpu.VMEM(const.shape, jnp.bfloat16) for const in consts],
            pltpu.VMEM((patch_rows, grid_cols * HALF, 2 * PATCH), jnp.float32),
            pltpu.VMEM((patch_rows, grid_cols, CROP // 2, TILE), jnp.float32),
            pltpu.VMEM((grid_cols, CROP // 2, TILE), jnp.float32),
            dma((1 + len(consts),)),
            dma((2,)),
            *[dma((tiles,)) for _ in range(9)],
            dma((2,)),
        ],
        compiler_params=pltpu.CompilerParams(
            collective_id=0, has_side_effects=True, vmem_limit_bytes=48 * 1024 * 1024
        ),
    )(tile, *[jnp.asarray(const) for const in consts])
    out = out.reshape(patch_rows, CROP // 2, grid_cols, TILE)
    return out.transpose(0, 2, 1, 3).reshape(1, patch_rows, grid_cols, CROP * CROP)


def solution(mesh):
    placed = (P(("blocks", "sec"), "pln", None),)
    return jax.shard_map(
        body,
        mesh=mesh,
        in_specs=placed,
        out_specs=P(("blocks", "sec"), "pln", None, None),
        check_vma=False,
    )
```

```python
import functools
import math

import jax
import jax.numpy as jnp
import numpy as np
from jax import lax
from jax.experimental import pallas as pl
from jax.experimental.pallas import tpu as pltpu
from jax.sharding import PartitionSpec as P

PATCH = 128
STRIDE = 64
CROP = 64
MARGIN = 32
HALF = 72
TILE = 128
MESH = pl.DeviceIdType.MESH


def split_table(table):
    high = np.asarray(table, np.float32).astype(jnp.bfloat16)
    low = (np.asarray(table, np.float32) - high.astype(np.float32)).astype(jnp.bfloat16)
    return high, low


def angles(left, right):
    return np.mod(np.outer(left, right), PATCH) * (2.0 * math.pi / PATCH)


def tables():
    spots = np.arange(PATCH)
    freqs = np.arange(PATCH // 2 + 1)
    lags = np.arange(CROP) - CROP // 2
    rows = np.zeros((2 * HALF, PATCH))
    rows[: len(freqs)] = np.cos(angles(freqs, spots))
    rows[HALF : HALF + len(freqs)] = -np.sin(angles(freqs, spots))
    rows_hi, rows_lo = split_table(rows)
    row_table = np.concatenate([rows_hi, rows_hi, rows_lo], axis=1)
    cos, sin = np.cos(angles(spots, spots)), np.sin(angles(spots, spots))
    cols_hi, cols_lo = split_table(np.block([[cos, -sin], [sin, cos]]))
    cos, sin = np.cos(angles(spots, lags)), np.sin(angles(spots, lags))
    none = np.zeros_like(cos)
    lag_hi, lag_lo = split_table(
        np.block(
            [
                [cos, none, sin, none],
                [-sin, none, cos, none],
                [none, cos, none, sin],
                [none, -sin, none, cos],
            ]
        )
    )
    order = np.concatenate([lags[0::2], lags[1::2]])
    weight = np.where((freqs == 0) | (freqs == PATCH // 2), 1.0, 2.0) / PATCH**3
    ups = np.zeros((CROP, 2 * HALF))
    ups[:, : len(freqs)] = np.cos(angles(order, freqs)) * weight
    ups[:, HALF : HALF + len(freqs)] = -np.sin(angles(order, freqs)) * weight
    ups_hi, ups_lo = split_table(ups)
    up_table = np.concatenate([ups_hi, ups_hi, ups_lo], axis=1)
    return row_table, cols_hi, cols_lo, lag_hi, lag_lo, up_table


def halves(value):
    high = value.astype(jnp.bfloat16)
    return high, (value - high.astype(jnp.float32)).astype(jnp.bfloat16)


def dot(left, right):
    return jnp.dot(left, right, preferred_element_type=jnp.float32)


def kernel(
    n_sec, x_hbm, row_hbm, chi_hbm, clo_hbm, lhi_hbm, llo_hbm, up_hbm, o_ref,
    field, row_t, chi_t, clo_t, lhi_t, llo_t, up_t, spec, agreed, rim,
    load_sem, halo_sem, one_send, two_send, relay_send, one_recv, two_recv,
    fwd_send, fwd_recv, rim_send, rim_recv,
):
    rows, cols = x_hbm.shape
    tiles = cols // TILE
    patch_rows, grid_cols = rows // STRIDE, cols // STRIDE
    s, p = lax.axis_index("sec"), lax.axis_index("pln")
    other = 1 - p
    odd = lax.rem(s, 2) == 1
    has_one, has_two = s >= 1, s >= 2
    edge = pl.multiple_of(other * (rows - MARGIN), MARGIN)
    rest = pl.multiple_of(p * MARGIN, MARGIN)
    far = pl.multiple_of(p * (rows + MARGIN), MARGIN)

    loads = [
        pltpu.make_async_copy(src, dst, load_sem.at[n])
        for n, (src, dst) in enumerate(
            [
                (x_hbm, field.at[0, pl.ds(MARGIN, rows), :]),
                (row_hbm, row_t), (chi_hbm, chi_t), (clo_hbm, clo_t),
                (lhi_hbm, lhi_t), (llo_hbm, llo_t), (up_hbm, up_t),
            ]
        )
    ]
    for load in loads:
        load.start()

    barrier = pltpu.get_barrier_semaphore()
    count = jnp.int32(1)
    pl.semaphore_signal(barrier, inc=1, device_id={"pln": other}, device_id_type=MESH)
    for step in (-2, -1, 1, 2):
        there = jnp.logical_and(s + step >= 0, s + step < n_sec)
        count = count + there.astype(jnp.int32)

        @pl.when(there)
        def _(step=step):
            pl.semaphore_signal(barrier, inc=1, device_id={"sec": s + step}, device_id_type=MESH)

    pl.semaphore_wait(barrier, count)

    def remote(src, dst, send, recv, where):
        return pltpu.make_async_remote_copy(
            src_ref=src, dst_ref=dst, send_sem=send, recv_sem=recv,
            device_id=where, device_id_type=MESH,
        )

    def wrapped(step):
        return {"sec": lax.rem(s + step + n_sec, n_sec)}

    def piece(ref, t, shift):
        if t == tiles:
            return ref.at[pl.ds(pl.multiple_of(edge + shift, MARGIN), MARGIN), :]
        return ref.at[
            pl.ds(pl.multiple_of(rest + shift, MARGIN), rows - MARGIN), pl.ds(t * TILE, TILE)
        ]

    def landed(d, t):
        return piece(field.at[d], t, MARGIN)

    def direct_one(t):
        return remote(piece(x_hbm, t, 0), landed(1, t), one_send.at[t], one_recv.at[t], wrapped(1))

    def direct_two(t):
        return remote(piece(x_hbm, t, 0), landed(2, t), two_send.at[t], two_recv.at[t], wrapped(2))

    def relay(t):
        return remote(landed(2, t), landed(1, t), relay_send.at[t], one_recv.at[t], wrapped(-1))

    def forward(d):
        return remote(
            landed(d, tiles), field.at[d, pl.ds(far, MARGIN), :],
            fwd_send.at[d - 1], fwd_recv.at[d - 1], {"pln": other},
        )

    halo = remote(
        piece(x_hbm, tiles, 0), field.at[0, pl.ds(far, MARGIN), :],
        halo_sem.at[0], halo_sem.at[1], {"pln": other},
    )
    order = [tiles, *range(tiles)]
    gives_one = jnp.logical_and(jnp.logical_not(odd), s + 1 < n_sec)
    gives_two = s + 2 < n_sec
    relays = jnp.logical_and(odd, s >= 3)

    @pl.when(gives_two)
    def _():
        for t in order:
            direct_two(t).start()

    @pl.when(gives_one)
    def _():
        for t in order:
            direct_one(t).start()

    halo.start()

    for d in range(3):
        field[d, pl.ds(far, MARGIN), :] = jnp.zeros((MARGIN, cols), jnp.float32)
    for d, here in ((1, has_one), (2, has_two)):

        @pl.when(jnp.logical_not(here))
        def _(d=d):
            field[d] = jnp.zeros(field.shape[1:], jnp.float32)

    lane = lax.broadcasted_iota(jnp.int32, (2 * HALF, TILE), 1)
    left = lax.broadcasted_iota(jnp.int32, (CROP // 2, TILE), 1) < CROP
    zero = jnp.zeros((2 * HALF, TILE), jnp.float32)

    def strips_of(d, i, t, count):
        slab = field[d, pl.ds(pl.multiple_of(i * STRIDE, STRIDE), PATCH), pl.ds(t * TILE, count * TILE)]
        return slab

    def row_transform(slab):
        high, low = halves(slab)
        wide = dot(row_t[...], jnp.concatenate([high, low, high], axis=0))
        return [wide[:, n * TILE : (n + 1) * TILE] for n in range(slab.shape[1] // TILE)]

    def window(parts, j):
        t = j // 2
        if j % 2 == 0:
            before = parts[t - 1] if t > 0 else zero
            picked = jnp.where(lane < PATCH - MARGIN, parts[t], before)
        else:
            after = parts[t + 1] if t + 1 < tiles else zero
            picked = jnp.where(lane >= MARGIN, parts[t], after)
        return jnp.concatenate([picked[:HALF], picked[HALF:]], axis=1)

    def col_transform(windows):
        high, low = halves(jnp.concatenate(windows, axis=0))
        return dot(high, chi_t[...]) + dot(low, chi_t[...]) + dot(high, clo_t[...])

    def cross(own, back):
        own_re, own_im = own[:, :PATCH], own[:, PATCH:]
        back_re, back_im = back[:, :PATCH], back[:, PATCH:]
        return [own_re * back_re + own_im * back_im, own_im * back_re - own_re * back_im]

    def surfaces_of(own, back):
        both = jnp.concatenate(
            cross(own, back[: own.shape[0]]) + cross(own, back[own.shape[0] :]), axis=1
        )
        high, low = halves(both)
        half = dot(high, lhi_t[...]) + dot(low, lhi_t[...]) + dot(high, llo_t[...])
        columns = [
            jnp.concatenate([half[n : n + HALF, :TILE], half[n : n + HALF, TILE:]], axis=0)
            for n in range(0, half.shape[0], HALF)
        ]
        high, low = halves(jnp.concatenate(columns, axis=1))
        wide = dot(up_t[...], jnp.concatenate([high, low, high], axis=0))
        joined = []
        for n in range(len(columns)):
            here = wide[:, n * TILE : (n + 1) * TILE]
            there = pltpu.roll(here, CROP, 1)
            both = here + there + here * there
            joined.append(jnp.where(left, both[: CROP // 2], both[CROP // 2 :]))
        return joined

    for load in loads:
        load.wait()
    halo.wait_recv()
    for i in range(patch_rows):
        parts = row_transform(strips_of(0, i, 0, tiles))
        spec[i] = col_transform([window(parts, j) for j in range(grid_cols)])

    def take_two(t):
        @pl.when(has_two)
        def _():
            direct_two(t).wait_recv()

        @pl.when(relays)
        def _():
            relay(t).start()

    def take_one(t):
        @pl.when(has_one)
        def _():
            direct_one(t).wait_recv()

    take_two(tiles)

    @pl.when(has_two)
    def _():
        forward(2).start()

    take_two(0)
    take_one(tiles)

    @pl.when(has_one)
    def _():
        forward(1).start()

    rim_row = (patch_rows - 1) * other
    parts = [[[], []] for _ in range(patch_rows)]
    done = []

    def send_rim(n):
        span = pl.ds(done[n][0], len(done[n]))
        return remote(
            agreed.at[rim_row, span], rim.at[span], rim_send.at[n], rim_recv.at[n], {"pln": other}
        )

    for t in range(tiles):
        if t + 1 < tiles:
            take_two(t + 1)
        take_one(t)
        if t == 0:
            for d, here in ((1, has_one), (2, has_two)):

                @pl.when(here)
                def _(d=d):
                    forward(d).wait_recv()

        first = 2 * t - 1 if t > 0 else 0
        ready = range(first, 2 * t + 1 if t + 1 < tiles else grid_cols)
        slabs = [strips_of(d, i, t, 1) for i in range(patch_rows) for d in (1, 2)]
        wide = row_transform(jnp.concatenate(slabs, axis=1))
        for i in range(patch_rows):
            for d in range(2):
                parts[i][d].append(wide[2 * i + d])
        done.append(ready)
        windows = [
            window(parts[i][d], j) for d in range(2) for i in range(patch_rows) for j in ready
        ]
        own = jnp.concatenate(
            [spec[i, pl.ds(ready[0] * HALF, len(ready) * HALF)] for i in range(patch_rows)], axis=0
        )
        joined = surfaces_of(own, col_transform(windows))
        for i in range(patch_rows):
            for n, j in enumerate(ready):
                agreed[i, j] = joined[i * len(ready) + n]
        send_rim(t).start()

    for t in range(tiles):
        send_rim(t).wait_recv()
    above = (p == 1).astype(jnp.float32)
    below = (p == 0).astype(jnp.float32)
    nothing = jnp.zeros((CROP // 2, TILE), jnp.float32)
    for i in range(patch_rows):
        stacked = [nothing]
        for j in range(grid_cols):
            up = agreed[i - 1, j] if i > 0 else rim[j] * above
            down = agreed[i + 1, j] if i < patch_rows - 1 else rim[j] * below
            stacked.append(up + 2.0 * agreed[i, j] + down)
        stacked.append(nothing)
        for j in range(grid_cols):
            o_ref[i, pl.ds(j, CROP // 2, stride=grid_cols), :] = (
                stacked[j] + 2.0 * stacked[j + 1] + stacked[j + 2]
            ) * (1.0 / 16.0)

    halo.wait_send()
    for t in range(tiles):
        send_rim(t).wait_send()
    for held, copy in ((gives_two, direct_two), (gives_one, direct_one), (relays, relay)):

        @pl.when(held)
        def _(copy=copy):
            for t in order:
                copy(t).wait_send()

    for d, here in ((1, has_one), (2, has_two)):

        @pl.when(here)
        def _(d=d):
            forward(d).wait_send()


def body(section_tiles):
    tile = section_tiles[0]
    rows, cols = tile.shape
    n_sec, n_pln = lax.axis_size("sec"), lax.axis_size("pln")
    assert n_pln == 2 and n_sec % 2 == 0 and cols % TILE == 0
    patch_rows, grid_cols, tiles = rows // STRIDE, cols // STRIDE, cols // TILE
    consts = tables()
    dma = pltpu.SemaphoreType.DMA
    out = pl.pallas_call(
        functools.partial(kernel, n_sec),
        out_shape=jax.ShapeDtypeStruct((patch_rows, CROP // 2 * grid_cols, TILE), jnp.float32),
        in_specs=[pl.BlockSpec(memory_space=pl.ANY)] * (1 + len(consts)),
        out_specs=pl.BlockSpec(memory_space=pltpu.VMEM),
        scratch_shapes=[
            pltpu.VMEM((3, rows + 2 * MARGIN, cols), jnp.float32),
            *[pltpu.VMEM(const.shape, jnp.bfloat16) for const in consts],
            pltpu.VMEM((patch_rows, grid_cols * HALF, 2 * PATCH), jnp.float32),
            pltpu.VMEM((patch_rows, grid_cols, CROP // 2, TILE), jnp.float32),
            pltpu.VMEM((grid_cols, CROP // 2, TILE), jnp.float32),
            dma((1 + len(consts),)),
            dma((2,)),
            *[dma((tiles + 1,)) for _ in range(5)],
            *[dma((2,)) for _ in range(2)],
            *[dma((tiles,)) for _ in range(2)],
        ],
        compiler_params=pltpu.CompilerParams(
            collective_id=0, has_side_effects=True, vmem_limit_bytes=67043328
        ),
    )(tile, *[jnp.asarray(const) for const in consts])
    out = out.reshape(patch_rows, CROP // 2, grid_cols, TILE)
    return out.transpose(0, 2, 1, 3).reshape(1, patch_rows, grid_cols, CROP * CROP)


def solution(mesh):
    placed = (P(("blocks", "sec"), "pln", None),)
    return jax.shard_map(
        body,
        mesh=mesh,
        in_specs=placed,
        out_specs=P(("blocks", "sec"), "pln", None, None),
        check_vma=False,
    )
```

```python
import functools
import math

import jax
import jax.numpy as jnp
import numpy as np
from jax import lax
from jax.experimental import pallas as pl
from jax.experimental.pallas import tpu as pltpu
from jax.sharding import PartitionSpec as P

PATCH = 128
STRIDE = 64
CROP = 64
MARGIN = 32
HALF = 72
TILE = 128
MESH = pl.DeviceIdType.MESH


def split_table(table):
    high = np.asarray(table, np.float32).astype(jnp.bfloat16)
    low = (np.asarray(table, np.float32) - high.astype(np.float32)).astype(jnp.bfloat16)
    return high, low


def angles(left, right):
    return np.mod(np.outer(left, right), PATCH) * (2.0 * math.pi / PATCH)


def tables():
    spots = np.arange(PATCH)
    freqs = np.arange(PATCH // 2 + 1)
    lags = np.arange(CROP) - CROP // 2
    rows = np.zeros((2 * HALF, PATCH))
    rows[: len(freqs)] = np.cos(angles(freqs, spots))
    rows[HALF : HALF + len(freqs)] = -np.sin(angles(freqs, spots))
    rows_hi, rows_lo = split_table(rows)
    row_table = np.concatenate([rows_hi, rows_hi, rows_lo], axis=1)
    cos, sin = np.cos(angles(spots, spots)), np.sin(angles(spots, spots))
    cols_hi, cols_lo = split_table(np.block([[cos, -sin], [sin, cos]]))
    cos, sin = np.cos(angles(spots, lags)), np.sin(angles(spots, lags))
    none = np.zeros_like(cos)
    lag_hi, lag_lo = split_table(
        np.block(
            [
                [cos, none, sin, none],
                [-sin, none, cos, none],
                [none, cos, none, sin],
                [none, -sin, none, cos],
            ]
        )
    )
    order = np.concatenate([lags[0::2], lags[1::2]])
    weight = np.where((freqs == 0) | (freqs == PATCH // 2), 1.0, 2.0) / PATCH**3
    ups = np.zeros((CROP, 2 * HALF))
    ups[:, : len(freqs)] = np.cos(angles(order, freqs)) * weight
    ups[:, HALF : HALF + len(freqs)] = -np.sin(angles(order, freqs)) * weight
    ups_hi, ups_lo = split_table(ups)
    up_table = np.concatenate([ups_hi, ups_hi, ups_lo], axis=1)
    return row_table, cols_hi, cols_lo, lag_hi, lag_lo, up_table


def halves(value):
    high = value.astype(jnp.bfloat16)
    return high, (value - high.astype(jnp.float32)).astype(jnp.bfloat16)


def dot(left, right):
    return jnp.dot(left, right, preferred_element_type=jnp.float32)


def kernel(
    n_sec, x_hbm, row_hbm, chi_hbm, clo_hbm, lhi_hbm, llo_hbm, up_hbm, o_ref,
    field, row_t, chi_t, clo_t, lhi_t, llo_t, up_t, spec, agreed, rim,
    load_sem, halo_sem, one_send, two_send, relay_send, one_recv, two_recv,
    fwd_send, fwd_recv, rim_send, rim_recv,
):
    rows, cols = x_hbm.shape
    tiles = cols // TILE
    patch_rows, grid_cols = rows // STRIDE, cols // STRIDE
    s, p = lax.axis_index("sec"), lax.axis_index("pln")
    other = 1 - p
    odd = lax.rem(s, 2) == 1
    has_one, has_two = s >= 1, s >= 2
    edge = pl.multiple_of(other * (rows - MARGIN), MARGIN)
    rest = pl.multiple_of(p * MARGIN, MARGIN)
    far = pl.multiple_of(p * (rows + MARGIN), MARGIN)

    loads = [
        pltpu.make_async_copy(src, dst, load_sem.at[n])
        for n, (src, dst) in enumerate(
            [
                (x_hbm, field.at[0, pl.ds(MARGIN, rows), :]),
                (row_hbm, row_t), (chi_hbm, chi_t), (clo_hbm, clo_t),
                (lhi_hbm, lhi_t), (llo_hbm, llo_t), (up_hbm, up_t),
            ]
        )
    ]
    for load in loads:
        load.start()

    barrier = pltpu.get_barrier_semaphore()
    count = jnp.int32(1)
    pl.semaphore_signal(barrier, inc=1, device_id={"pln": other}, device_id_type=MESH)
    for step in (-2, -1, 1, 2):
        there = jnp.logical_and(s + step >= 0, s + step < n_sec)
        count = count + there.astype(jnp.int32)

        @pl.when(there)
        def _(step=step):
            pl.semaphore_signal(barrier, inc=1, device_id={"sec": s + step}, device_id_type=MESH)

    pl.semaphore_wait(barrier, count)

    def remote(src, dst, send, recv, where):
        return pltpu.make_async_remote_copy(
            src_ref=src, dst_ref=dst, send_sem=send, recv_sem=recv,
            device_id=where, device_id_type=MESH,
        )

    def wrapped(step):
        return {"sec": lax.rem(s + step + n_sec, n_sec)}

    def piece(ref, t, shift):
        if t == tiles:
            return ref.at[pl.ds(pl.multiple_of(edge + shift, MARGIN), MARGIN), :]
        return ref.at[
            pl.ds(pl.multiple_of(rest + shift, MARGIN), rows - MARGIN), pl.ds(t * TILE, TILE)
        ]

    def landed(d, t):
        return piece(field.at[d], t, MARGIN)

    def direct_one(t):
        return remote(piece(x_hbm, t, 0), landed(1, t), one_send.at[t], one_recv.at[t], wrapped(1))

    def direct_two(t):
        return remote(piece(x_hbm, t, 0), landed(2, t), two_send.at[t], two_recv.at[t], wrapped(2))

    def relay(t):
        return remote(landed(2, t), landed(1, t), relay_send.at[t], one_recv.at[t], wrapped(-1))

    def forward(d):
        return remote(
            landed(d, tiles), field.at[d, pl.ds(far, MARGIN), :],
            fwd_send.at[d - 1], fwd_recv.at[d - 1], {"pln": other},
        )

    halo = remote(
        piece(x_hbm, tiles, 0), field.at[0, pl.ds(far, MARGIN), :],
        halo_sem.at[0], halo_sem.at[1], {"pln": other},
    )
    order = [tiles, *range(tiles)]
    gives_one = jnp.logical_and(jnp.logical_not(odd), s + 1 < n_sec)
    gives_two = s + 2 < n_sec
    relays = jnp.logical_and(odd, s >= 3)

    @pl.when(gives_two)
    def _():
        for t in order:
            direct_two(t).start()

    @pl.when(gives_one)
    def _():
        for t in order:
            direct_one(t).start()

    halo.start()

    for d in range(3):
        field[d, pl.ds(far, MARGIN), :] = jnp.zeros((MARGIN, cols), jnp.float32)
    for d, here in ((1, has_one), (2, has_two)):

        @pl.when(jnp.logical_not(here))
        def _(d=d):
            field[d] = jnp.zeros(field.shape[1:], jnp.float32)

    lane = lax.broadcasted_iota(jnp.int32, (2 * HALF, TILE), 1)
    left = lax.broadcasted_iota(jnp.int32, (CROP // 2, TILE), 1) < CROP
    zero = jnp.zeros((2 * HALF, TILE), jnp.float32)

    def strip(d, i, t, count):
        return field[d, pl.ds(i * STRIDE, PATCH), pl.ds(t * TILE, count * TILE)]

    def row_transform(slab):
        high, low = halves(slab)
        wide = dot(row_t[...], jnp.concatenate([high, low, high], axis=0))
        return [wide[:, n * TILE : (n + 1) * TILE] for n in range(slab.shape[1] // TILE)]

    def window(parts, j):
        t = j // 2
        if j % 2 == 0:
            before = parts[t - 1] if t > 0 else zero
            picked = jnp.where(lane < PATCH - MARGIN, parts[t], before)
        else:
            after = parts[t + 1] if t + 1 < tiles else zero
            picked = jnp.where(lane >= MARGIN, parts[t], after)
        return jnp.concatenate([picked[:HALF], picked[HALF:]], axis=1)

    def col_transform(windows):
        high, low = halves(jnp.concatenate(windows, axis=0))
        return dot(high, chi_t[...]) + dot(low, chi_t[...]) + dot(high, clo_t[...])

    def cross(own, back):
        own_re, own_im = own[:, :PATCH], own[:, PATCH:]
        back_re, back_im = back[:, :PATCH], back[:, PATCH:]
        return [own_re * back_re + own_im * back_im, own_im * back_re - own_re * back_im]

    def surfaces_of(own, one, two):
        both = jnp.concatenate(cross(own, one) + cross(own, two), axis=1)
        high, low = halves(both)
        half = dot(high, lhi_t[...]) + dot(low, lhi_t[...]) + dot(high, llo_t[...])
        columns = [
            jnp.concatenate([half[n : n + HALF, :TILE], half[n : n + HALF, TILE:]], axis=0)
            for n in range(0, half.shape[0], HALF)
        ]
        high, low = halves(jnp.concatenate(columns, axis=1))
        wide = dot(up_t[...], jnp.concatenate([high, low, high], axis=0))
        joined = []
        for n in range(len(columns)):
            here = wide[:, n * TILE : (n + 1) * TILE]
            there = pltpu.roll(here, CROP, 1)
            both = here + there + here * there
            joined.append(jnp.where(left, both[: CROP // 2], both[CROP // 2 :]))
        return joined

    def spectrum(d, i):
        parts = row_transform(strip(d, i, 0, tiles))
        return col_transform([window(parts, j) for j in range(grid_cols)])

    def take_two(t, relayed):
        direct_two(t).wait_recv()
        if relayed:
            relay(t).start()
        if t == tiles:
            forward(2).start()

    for load in loads:
        load.wait()
    halo.wait_recv()
    for i in range(patch_rows):
        spec[0, i] = spectrum(0, i)
        early = order[:2] if i == 0 else order[2:]

        @pl.when(relays)
        def _(early=early):
            for t in early:
                take_two(t, True)

    @pl.when(jnp.logical_and(has_two, jnp.logical_not(relays)))
    def _():
        for t in order:
            take_two(t, False)

    @pl.when(has_one)
    def _():
        direct_one(tiles).wait_recv()
        forward(1).start()

    @pl.when(has_two)
    def _():
        forward(2).wait_recv()

    for i in range(patch_rows):
        spec[1, i] = spectrum(2, i)

    rim_row = (patch_rows - 1) * other
    parts = [[] for _ in range(patch_rows)]
    groups = [range(tiles - 1), range(tiles - 1, tiles)] if tiles > 1 else [range(tiles)]
    spans = []

    def send_rim(n):
        span = pl.ds(spans[n][0], len(spans[n]))
        return remote(
            agreed.at[rim_row, span], rim.at[span], rim_send.at[n], rim_recv.at[n], {"pln": other}
        )

    for n, group in enumerate(groups):

        @pl.when(has_one)
        def _(group=group, n=n):
            for t in group:
                direct_one(t).wait_recv()
            if n == 0:
                forward(1).wait_recv()

        final = n + 1 == len(groups)
        ready = range(
            2 * group[0] - 1 if n > 0 else 0, grid_cols if final else 2 * group[-1] + 1
        )
        spans.append(ready)
        slabs = [strip(1, i, group[0], len(group)) for i in range(patch_rows)]
        wide = row_transform(jnp.concatenate(slabs, axis=1))
        for i in range(patch_rows):
            parts[i] += wide[i * len(group) : (i + 1) * len(group)]
        windows = [window(parts[i], j) for i in range(patch_rows) for j in ready]
        own, two = (
            jnp.concatenate(
                [spec[m, i, pl.ds(ready[0] * HALF, len(ready) * HALF)] for i in range(patch_rows)],
                axis=0,
            )
            for m in range(2)
        )
        joined = surfaces_of(own, col_transform(windows), two)
        for i in range(patch_rows):
            for m, j in enumerate(ready):
                agreed[i, j] = joined[i * len(ready) + m]
        send_rim(n).start()

    for n in range(len(groups)):
        send_rim(n).wait_recv()
    above = (p == 1).astype(jnp.float32)
    below = (p == 0).astype(jnp.float32)
    nothing = jnp.zeros((CROP // 2, TILE), jnp.float32)
    for i in range(patch_rows):
        stacked = [nothing]
        for j in range(grid_cols):
            up = agreed[i - 1, j] if i > 0 else rim[j] * above
            down = agreed[i + 1, j] if i < patch_rows - 1 else rim[j] * below
            stacked.append(up + 2.0 * agreed[i, j] + down)
        stacked.append(nothing)
        for j in range(grid_cols):
            o_ref[i, pl.ds(j, CROP // 2, stride=grid_cols), :] = (
                stacked[j] + 2.0 * stacked[j + 1] + stacked[j + 2]
            ) * (1.0 / 16.0)

    halo.wait_send()
    for n in range(len(groups)):
        send_rim(n).wait_send()
    for held, copy in ((gives_two, direct_two), (gives_one, direct_one), (relays, relay)):

        @pl.when(held)
        def _(copy=copy):
            for t in order:
                copy(t).wait_send()

    for d, here in ((1, has_one), (2, has_two)):

        @pl.when(here)
        def _(d=d):
            forward(d).wait_send()


def body(section_tiles):
    tile = section_tiles[0]
    rows, cols = tile.shape
    n_sec, n_pln = lax.axis_size("sec"), lax.axis_size("pln")
    assert n_pln == 2 and n_sec % 2 == 0 and cols % TILE == 0
    patch_rows, grid_cols, tiles = rows // STRIDE, cols // STRIDE, cols // TILE
    consts = tables()
    dma = pltpu.SemaphoreType.DMA
    out = pl.pallas_call(
        functools.partial(kernel, n_sec),
        out_shape=jax.ShapeDtypeStruct((patch_rows, CROP // 2 * grid_cols, TILE), jnp.float32),
        in_specs=[pl.BlockSpec(memory_space=pl.ANY)] * (1 + len(consts)),
        out_specs=pl.BlockSpec(memory_space=pltpu.VMEM),
        scratch_shapes=[
            pltpu.VMEM((3, rows + 2 * MARGIN, cols), jnp.float32),
            *[pltpu.VMEM(const.shape, jnp.bfloat16) for const in consts],
            pltpu.VMEM((2, patch_rows, grid_cols * HALF, 2 * PATCH), jnp.float32),
            pltpu.VMEM((patch_rows, grid_cols, CROP // 2, TILE), jnp.float32),
            pltpu.VMEM((grid_cols, CROP // 2, TILE), jnp.float32),
            dma((1 + len(consts),)),
            dma((2,)),
            *[dma((tiles + 1,)) for _ in range(5)],
            *[dma((2,)) for _ in range(2)],
            *[dma((tiles,)) for _ in range(2)],
        ],
        compiler_params=pltpu.CompilerParams(
            collective_id=0, has_side_effects=True, vmem_limit_bytes=67043328
        ),
    )(tile, *[jnp.asarray(const) for const in consts])
    out = out.reshape(patch_rows, CROP // 2, grid_cols, TILE)
    return out.transpose(0, 2, 1, 3).reshape(1, patch_rows, grid_cols, CROP * CROP)


def solution(mesh):
    placed = (P(("blocks", "sec"), "pln", None),)
    return jax.shard_map(
        body,
        mesh=mesh,
        in_specs=placed,
        out_specs=P(("blocks", "sec"), "pln", None, None),
        check_vma=False,
    )
```

```python
import functools
import math

import jax
import jax.numpy as jnp
import numpy as np
from jax import lax
from jax.experimental import pallas as pl
from jax.experimental.pallas import tpu as pltpu
from jax.sharding import PartitionSpec as P

PATCH = 128
STRIDE = 64
CROP = 64
MARGIN = 32
HALF = 72
TILE = 128
MESH = pl.DeviceIdType.MESH


def split_table(table):
    high = np.asarray(table, np.float32).astype(jnp.bfloat16)
    low = (np.asarray(table, np.float32) - high.astype(np.float32)).astype(jnp.bfloat16)
    return high, low


def angles(left, right):
    return np.mod(np.outer(left, right), PATCH) * (2.0 * math.pi / PATCH)


def tables():
    spots = np.arange(PATCH)
    freqs = np.arange(PATCH // 2 + 1)
    lags = np.arange(CROP) - CROP // 2
    rows = np.zeros((2 * HALF, PATCH))
    rows[: len(freqs)] = np.cos(angles(freqs, spots))
    rows[HALF : HALF + len(freqs)] = -np.sin(angles(freqs, spots))
    rows_hi, rows_lo = split_table(rows)
    row_table = np.concatenate([rows_hi, rows_hi, rows_lo], axis=1)
    cos, sin = np.cos(angles(spots, spots)), np.sin(angles(spots, spots))
    cols_hi, cols_lo = split_table(np.block([[cos, -sin], [sin, cos]]))
    cos, sin = np.cos(angles(spots, lags)), np.sin(angles(spots, lags))
    none = np.zeros_like(cos)
    lag_hi, lag_lo = split_table(
        np.block(
            [
                [cos, none, sin, none],
                [-sin, none, cos, none],
                [none, cos, none, sin],
                [none, -sin, none, cos],
            ]
        )
    )
    order = np.concatenate([lags[0::2], lags[1::2]])
    weight = np.where((freqs == 0) | (freqs == PATCH // 2), 1.0, 2.0) / PATCH**3
    ups = np.zeros((CROP, 2 * HALF))
    ups[:, : len(freqs)] = np.cos(angles(order, freqs)) * weight
    ups[:, HALF : HALF + len(freqs)] = -np.sin(angles(order, freqs)) * weight
    ups_hi, ups_lo = split_table(ups)
    up_table = np.concatenate([ups_hi, ups_hi, ups_lo], axis=1)
    return row_table, cols_hi, cols_lo, lag_hi, lag_lo, up_table


def halves(value):
    high = value.astype(jnp.bfloat16)
    return high, (value - high.astype(jnp.float32)).astype(jnp.bfloat16)


def dot(left, right):
    return jnp.dot(left, right, preferred_element_type=jnp.float32)


def kernel(
    n_sec, x_hbm, row_hbm, chi_hbm, clo_hbm, lhi_hbm, llo_hbm, up_hbm, o_ref,
    field, row_t, chi_t, clo_t, lhi_t, llo_t, up_t, spec, agreed, rim,
    load_sem, halo_sem, one_send, two_send, relay_send, one_recv, two_recv,
    fwd_send, fwd_recv, rim_send, rim_recv,
):
    rows, cols = x_hbm.shape
    tiles = cols // TILE
    patch_rows, grid_cols = rows // STRIDE, cols // STRIDE
    s, p = lax.axis_index("sec"), lax.axis_index("pln")
    other = 1 - p
    odd = lax.rem(s, 2) == 1
    has_one, has_two = s >= 1, s >= 2
    edge = pl.multiple_of(other * (rows - MARGIN), MARGIN)
    rest = pl.multiple_of(p * MARGIN, MARGIN)
    far = pl.multiple_of(p * (rows + MARGIN), MARGIN)

    loads = [
        pltpu.make_async_copy(src, dst, load_sem.at[n])
        for n, (src, dst) in enumerate(
            [
                (x_hbm, field.at[0, pl.ds(MARGIN, rows), :]),
                (row_hbm, row_t), (chi_hbm, chi_t), (clo_hbm, clo_t),
                (lhi_hbm, lhi_t), (llo_hbm, llo_t), (up_hbm, up_t),
            ]
        )
    ]
    for load in loads:
        load.start()

    barrier = pltpu.get_barrier_semaphore()
    count = jnp.int32(1)
    pl.semaphore_signal(barrier, inc=1, device_id={"pln": other}, device_id_type=MESH)
    for step in (-2, -1, 1, 2):
        there = jnp.logical_and(s + step >= 0, s + step < n_sec)
        count = count + there.astype(jnp.int32)

        @pl.when(there)
        def _(step=step):
            pl.semaphore_signal(barrier, inc=1, device_id={"sec": s + step}, device_id_type=MESH)

    pl.semaphore_wait(barrier, count)

    def remote(src, dst, send, recv, where):
        return pltpu.make_async_remote_copy(
            src_ref=src, dst_ref=dst, send_sem=send, recv_sem=recv,
            device_id=where, device_id_type=MESH,
        )

    def wrapped(step):
        return {"sec": lax.rem(s + step + n_sec, n_sec)}

    def piece(ref, t, shift):
        if t == tiles:
            return ref.at[pl.ds(pl.multiple_of(edge + shift, MARGIN), MARGIN), :]
        return ref.at[
            pl.ds(pl.multiple_of(rest + shift, MARGIN), rows - MARGIN), pl.ds(t * TILE, TILE)
        ]

    def landed(d, t):
        return piece(field.at[d], t, MARGIN)

    def direct_one(t):
        return remote(piece(x_hbm, t, 0), landed(1, t), one_send.at[t], one_recv.at[t], wrapped(1))

    def direct_two(t):
        return remote(piece(x_hbm, t, 0), landed(2, t), two_send.at[t], two_recv.at[t], wrapped(2))

    def relay(t):
        return remote(landed(2, t), landed(1, t), relay_send.at[t], one_recv.at[t], wrapped(-1))

    def forward(d):
        return remote(
            landed(d, tiles), field.at[d, pl.ds(far, MARGIN), :],
            fwd_send.at[d - 1], fwd_recv.at[d - 1], {"pln": other},
        )

    halo = remote(
        piece(x_hbm, tiles, 0), field.at[0, pl.ds(far, MARGIN), :],
        halo_sem.at[0], halo_sem.at[1], {"pln": other},
    )
    order = [tiles, *range(tiles)]
    gives_one = jnp.logical_and(jnp.logical_not(odd), s + 1 < n_sec)
    gives_two = s + 2 < n_sec
    relays = jnp.logical_and(odd, s >= 3)

    @pl.when(gives_two)
    def _():
        for t in order:
            direct_two(t).start()

    @pl.when(gives_one)
    def _():
        for t in order:
            direct_one(t).start()

    halo.start()

    for d in range(3):
        field[d, pl.ds(far, MARGIN), :] = jnp.zeros((MARGIN, cols), jnp.float32)
    for d, here in ((1, has_one), (2, has_two)):

        @pl.when(jnp.logical_not(here))
        def _(d=d):
            field[d] = jnp.zeros(field.shape[1:], jnp.float32)

    lane = lax.broadcasted_iota(jnp.int32, (2 * HALF, TILE), 1)
    left = lax.broadcasted_iota(jnp.int32, (CROP // 2, TILE), 1) < CROP
    zero = jnp.zeros((2 * HALF, TILE), jnp.float32)

    def strip(d, i, t, count):
        return field[d, pl.ds(i * STRIDE, PATCH), pl.ds(t * TILE, count * TILE)]

    def row_transform(slab):
        high, low = halves(slab)
        wide = dot(row_t[...], jnp.concatenate([high, low, high], axis=0))
        return [wide[:, n * TILE : (n + 1) * TILE] for n in range(slab.shape[1] // TILE)]

    def window(parts, j):
        t = j // 2
        if j % 2 == 0:
            before = parts[t - 1] if t > 0 else zero
            picked = jnp.where(lane < PATCH - MARGIN, parts[t], before)
        else:
            after = parts[t + 1] if t + 1 < tiles else zero
            picked = jnp.where(lane >= MARGIN, parts[t], after)
        return jnp.concatenate([picked[:HALF], picked[HALF:]], axis=1)

    def col_transform(windows):
        high, low = halves(jnp.concatenate(windows, axis=0))
        return dot(high, chi_t[...]) + dot(low, chi_t[...]) + dot(high, clo_t[...])

    def cross(own, back):
        own_re, own_im = own[:, :PATCH], own[:, PATCH:]
        back_re, back_im = back[:, :PATCH], back[:, PATCH:]
        return [own_re * back_re + own_im * back_im, own_im * back_re - own_re * back_im]

    def surfaces_of(own, one, two):
        both = jnp.concatenate(cross(own, one) + cross(own, two), axis=1)
        high, low = halves(both)
        half = dot(high, lhi_t[...]) + dot(low, lhi_t[...]) + dot(high, llo_t[...])
        columns = [
            jnp.concatenate([half[n : n + HALF, :TILE], half[n : n + HALF, TILE:]], axis=0)
            for n in range(0, half.shape[0], HALF)
        ]
        high, low = halves(jnp.concatenate(columns, axis=1))
        wide = dot(up_t[...], jnp.concatenate([high, low, high], axis=0))
        joined = []
        for n in range(len(columns)):
            here = wide[:, n * TILE : (n + 1) * TILE]
            there = pltpu.roll(here, CROP, 1)
            both = here + there + here * there
            joined.append(jnp.where(left, both[: CROP // 2], both[CROP // 2 :]))
        return joined

    def spectrum(d, i):
        parts = row_transform(strip(d, i, 0, tiles))
        return col_transform([window(parts, j) for j in range(grid_cols)])

    def take_two(t, relayed):
        direct_two(t).wait_recv()
        if relayed:
            relay(t).start()
        if t == tiles:
            forward(2).start()

    for load in loads:
        load.wait()
    halo.wait_recv()
    for i in range(patch_rows):
        spec[0, i] = spectrum(0, i)
        early = order[:2] if i == 0 else order[2:]

        @pl.when(relays)
        def _(early=early):
            for t in early:
                take_two(t, True)

    @pl.when(jnp.logical_and(has_two, jnp.logical_not(relays)))
    def _():
        for t in order:
            take_two(t, False)

    @pl.when(has_one)
    def _():
        direct_one(tiles).wait_recv()
        forward(1).start()

    @pl.when(has_two)
    def _():
        forward(2).wait_recv()

    for i in range(patch_rows):
        spec[1, i] = spectrum(2, i)

    rim_row = (patch_rows - 1) * other
    parts = [[] for _ in range(patch_rows)]
    groups = [range(tiles - 1), range(tiles - 1, tiles)] if tiles > 1 else [range(tiles)]
    spans = []

    def send_rim(n):
        span = pl.ds(spans[n][0], len(spans[n]))
        return remote(
            agreed.at[rim_row, span], rim.at[span], rim_send.at[n], rim_recv.at[n], {"pln": other}
        )

    for n, group in enumerate(groups):

        @pl.when(has_one)
        def _(group=group, n=n):
            for t in group:
                direct_one(t).wait_recv()
            if n == 0:
                forward(1).wait_recv()

        final = n + 1 == len(groups)
        ready = range(
            2 * group[0] - 1 if n > 0 else 0, grid_cols if final else 2 * group[-1] + 1
        )
        spans.append(ready)
        slabs = [strip(1, i, group[0], len(group)) for i in range(patch_rows)]
        wide = row_transform(jnp.concatenate(slabs, axis=1))
        for i in range(patch_rows):
            parts[i] += wide[i * len(group) : (i + 1) * len(group)]
        windows = [window(parts[i], j) for i in range(patch_rows) for j in ready]
        own, two = (
            jnp.concatenate(
                [spec[m, i, pl.ds(ready[0] * HALF, len(ready) * HALF)] for i in range(patch_rows)],
                axis=0,
            )
            for m in range(2)
        )
        joined = surfaces_of(own, col_transform(windows), two)
        for i in range(patch_rows):
            for m, j in enumerate(ready):
                agreed[i, j] = joined[i * len(ready) + m]
        send_rim(n).start()

    for n in range(len(groups)):
        send_rim(n).wait_recv()
    above = (p == 1).astype(jnp.float32)
    below = (p == 0).astype(jnp.float32)
    nothing = jnp.zeros((CROP // 2, TILE), jnp.float32)
    for i in range(patch_rows):
        stacked = [nothing]
        for j in range(grid_cols):
            up = agreed[i - 1, j] if i > 0 else rim[j] * above
            down = agreed[i + 1, j] if i < patch_rows - 1 else rim[j] * below
            stacked.append(up + 2.0 * agreed[i, j] + down)
        stacked.append(nothing)
        for j in range(grid_cols):
            o_ref[i, pl.ds(j, CROP // 2, stride=grid_cols), :] = (
                stacked[j] + 2.0 * stacked[j + 1] + stacked[j + 2]
            ) * (1.0 / 16.0)

    halo.wait_send()
    for n in range(len(groups)):
        send_rim(n).wait_send()
    for held, copy in ((gives_two, direct_two), (gives_one, direct_one), (relays, relay)):

        @pl.when(held)
        def _(copy=copy):
            for t in order:
                copy(t).wait_send()

    for d, here in ((1, has_one), (2, has_two)):

        @pl.when(here)
        def _(d=d):
            forward(d).wait_send()


def body(section_tiles):
    tile = section_tiles[0]
    rows, cols = tile.shape
    n_sec, n_pln = lax.axis_size("sec"), lax.axis_size("pln")
    assert n_pln == 2 and n_sec % 2 == 0 and cols % TILE == 0
    patch_rows, grid_cols, tiles = rows // STRIDE, cols // STRIDE, cols // TILE
    consts = tables()
    dma = pltpu.SemaphoreType.DMA
    out = pl.pallas_call(
        functools.partial(kernel, n_sec),
        out_shape=pltpu.VMEM((patch_rows, CROP // 2 * grid_cols, TILE), jnp.float32),
        in_specs=[pl.BlockSpec(memory_space=pl.ANY)] * (1 + len(consts)),
        out_specs=pl.BlockSpec(memory_space=pltpu.VMEM),
        scratch_shapes=[
            pltpu.VMEM((3, rows + 2 * MARGIN, cols), jnp.float32),
            *[pltpu.VMEM(const.shape, jnp.bfloat16) for const in consts],
            pltpu.VMEM((2, patch_rows, grid_cols * HALF, 2 * PATCH), jnp.float32),
            pltpu.VMEM((patch_rows, grid_cols, CROP // 2, TILE), jnp.float32),
            pltpu.VMEM((grid_cols, CROP // 2, TILE), jnp.float32),
            dma((1 + len(consts),)),
            dma((2,)),
            *[dma((tiles + 1,)) for _ in range(5)],
            *[dma((2,)) for _ in range(2)],
            *[dma((tiles,)) for _ in range(2)],
        ],
        compiler_params=pltpu.CompilerParams(
            collective_id=0, has_side_effects=True, vmem_limit_bytes=67043328 - 530 * 1024
        ),
    )(tile, *[jnp.asarray(const) for const in consts])
    out = out.reshape(patch_rows, CROP // 2, grid_cols, TILE)
    return out.transpose(0, 2, 1, 3).reshape(1, patch_rows, grid_cols, CROP * CROP)


def solution(mesh):
    placed = (P(("blocks", "sec"), "pln", None),)
    return jax.shard_map(
        body,
        mesh=mesh,
        in_specs=placed,
        out_specs=P(("blocks", "sec"), "pln", None, None),
        check_vma=False,
    )
```

```python
import functools
import math

import jax
import jax.numpy as jnp
import numpy as np
from jax import lax
from jax.experimental import pallas as pl
from jax.experimental.pallas import tpu as pltpu
from jax.sharding import PartitionSpec as P

PATCH = 128
STRIDE = 64
CROP = 64
MARGIN = 32
HALF = 72
TILE = 128
MESH = pl.DeviceIdType.MESH


def split_table(table):
    high = np.asarray(table, np.float32).astype(jnp.bfloat16)
    low = (np.asarray(table, np.float32) - high.astype(np.float32)).astype(jnp.bfloat16)
    return high, low


def angles(left, right):
    return np.mod(np.outer(left, right), PATCH) * (2.0 * math.pi / PATCH)


def tables():
    spots = np.arange(PATCH)
    freqs = np.arange(PATCH // 2 + 1)
    lags = np.arange(CROP) - CROP // 2
    rows = np.zeros((2 * HALF, PATCH))
    rows[: len(freqs)] = np.cos(angles(freqs, spots))
    rows[HALF : HALF + len(freqs)] = -np.sin(angles(freqs, spots))
    rows_hi, rows_lo = split_table(rows)
    row_table = np.concatenate([rows_hi, rows_hi, rows_lo], axis=1)
    cos, sin = np.cos(angles(spots, spots)), np.sin(angles(spots, spots))
    cols_hi, cols_lo = split_table(np.block([[cos, -sin], [sin, cos]]))
    cos, sin = np.cos(angles(spots, lags)), np.sin(angles(spots, lags))
    none = np.zeros_like(cos)
    lag_hi, lag_lo = split_table(
        np.block(
            [
                [cos, none, sin, none],
                [-sin, none, cos, none],
                [none, cos, none, sin],
                [none, -sin, none, cos],
            ]
        )
    )
    order = np.concatenate([lags[0::2], lags[1::2]])
    weight = np.where((freqs == 0) | (freqs == PATCH // 2), 1.0, 2.0) / PATCH**3
    ups = np.zeros((CROP, 2 * HALF))
    ups[:, : len(freqs)] = np.cos(angles(order, freqs)) * weight
    ups[:, HALF : HALF + len(freqs)] = -np.sin(angles(order, freqs)) * weight
    ups_hi, ups_lo = split_table(ups)
    up_table = np.concatenate([ups_hi, ups_hi, ups_lo], axis=1)
    return row_table, cols_hi, cols_lo, lag_hi, lag_lo, up_table


def halves(value):
    high = value.astype(jnp.bfloat16)
    return high, (value - high.astype(jnp.float32)).astype(jnp.bfloat16)


def dot(left, right):
    return jnp.dot(left, right, preferred_element_type=jnp.float32)


def kernel(
    n_sec, x_hbm, row_hbm, chi_hbm, clo_hbm, lhi_hbm, llo_hbm, up_hbm, o_ref,
    field, row_t, chi_t, clo_t, lhi_t, llo_t, up_t, spec, agreed, rim,
    load_sem, halo_sem, one_send, two_send, relay_send, one_recv, two_recv,
    fwd_send, fwd_recv, rim_send, rim_recv,
):
    rows, cols = x_hbm.shape
    tiles = cols // TILE
    patch_rows, grid_cols = rows // STRIDE, cols // STRIDE
    s, p = lax.axis_index("sec"), lax.axis_index("pln")
    other = 1 - p
    odd = lax.rem(s, 2) == 1
    has_one, has_two = s >= 1, s >= 2
    edge = pl.multiple_of(other * (rows - MARGIN), MARGIN)
    rest = pl.multiple_of(p * MARGIN, MARGIN)
    far = pl.multiple_of(p * (rows + MARGIN), MARGIN)

    loads = [
        pltpu.make_async_copy(src, dst, load_sem.at[n])
        for n, (src, dst) in enumerate(
            [
                (x_hbm, field.at[0, pl.ds(MARGIN, rows), :]),
                (row_hbm, row_t), (chi_hbm, chi_t), (clo_hbm, clo_t),
                (lhi_hbm, lhi_t), (llo_hbm, llo_t), (up_hbm, up_t),
            ]
        )
    ]
    for load in loads:
        load.start()

    barrier = pltpu.get_barrier_semaphore()
    count = jnp.int32(1)
    pl.semaphore_signal(barrier, inc=1, device_id={"pln": other}, device_id_type=MESH)
    for step in (-2, -1, 1, 2):
        there = jnp.logical_and(s + step >= 0, s + step < n_sec)
        count = count + there.astype(jnp.int32)

        @pl.when(there)
        def _(step=step):
            pl.semaphore_signal(barrier, inc=1, device_id={"sec": s + step}, device_id_type=MESH)

    pl.semaphore_wait(barrier, count)

    def remote(src, dst, send, recv, where):
        return pltpu.make_async_remote_copy(
            src_ref=src, dst_ref=dst, send_sem=send, recv_sem=recv,
            device_id=where, device_id_type=MESH,
        )

    def wrapped(step):
        return {"sec": lax.rem(s + step + n_sec, n_sec)}

    def piece(ref, t, shift):
        if t == tiles:
            return ref.at[pl.ds(pl.multiple_of(edge + shift, MARGIN), MARGIN), :]
        return ref.at[
            pl.ds(pl.multiple_of(rest + shift, MARGIN), rows - MARGIN), pl.ds(t * TILE, TILE)
        ]

    def landed(d, t):
        return piece(field.at[d], t, MARGIN)

    def direct_one(t):
        return remote(piece(x_hbm, t, 0), landed(1, t), one_send.at[t], one_recv.at[t], wrapped(1))

    def direct_two(t):
        return remote(piece(x_hbm, t, 0), landed(2, t), two_send.at[t], two_recv.at[t], wrapped(2))

    def relay(t):
        return remote(landed(2, t), landed(1, t), relay_send.at[t], one_recv.at[t], wrapped(-1))

    def forward(d):
        return remote(
            landed(d, tiles), field.at[d, pl.ds(far, MARGIN), :],
            fwd_send.at[d - 1], fwd_recv.at[d - 1], {"pln": other},
        )

    halo = remote(
        piece(x_hbm, tiles, 0), field.at[0, pl.ds(far, MARGIN), :],
        halo_sem.at[0], halo_sem.at[1], {"pln": other},
    )
    order = [tiles, *range(tiles)]
    gives_one = jnp.logical_and(jnp.logical_not(odd), s + 1 < n_sec)
    gives_two = s + 2 < n_sec
    relays = jnp.logical_and(odd, s >= 3)

    @pl.when(gives_two)
    def _():
        for t in order:
            direct_two(t).start()

    @pl.when(gives_one)
    def _():
        for t in order:
            direct_one(t).start()

    halo.start()

    for d in range(3):
        field[d, pl.ds(far, MARGIN), :] = jnp.zeros((MARGIN, cols), jnp.float32)
    for d, here in ((1, has_one), (2, has_two)):

        @pl.when(jnp.logical_not(here))
        def _(d=d):
            field[d] = jnp.zeros(field.shape[1:], jnp.float32)

    lane = lax.broadcasted_iota(jnp.int32, (2 * HALF, TILE), 1)
    left = lax.broadcasted_iota(jnp.int32, (CROP // 2, TILE), 1) < CROP
    zero = jnp.zeros((2 * HALF, TILE), jnp.float32)

    def strip(d, i, t, count):
        return field[d, pl.ds(i * STRIDE, PATCH), pl.ds(t * TILE, count * TILE)]

    def row_transform(slab):
        high, low = halves(slab)
        wide = dot(row_t[...], jnp.concatenate([high, low, high], axis=0))
        return [wide[:, n * TILE : (n + 1) * TILE] for n in range(slab.shape[1] // TILE)]

    def window(parts, j):
        t = j // 2
        if j % 2 == 0:
            before = parts[t - 1] if t > 0 else zero
            picked = jnp.where(lane < PATCH - MARGIN, parts[t], before)
        else:
            after = parts[t + 1] if t + 1 < tiles else zero
            picked = jnp.where(lane >= MARGIN, parts[t], after)
        return jnp.concatenate([picked[:HALF], picked[HALF:]], axis=1)

    def col_transform(windows):
        high, low = halves(jnp.concatenate(windows, axis=0))
        return dot(high, chi_t[...]) + dot(low, chi_t[...]) + dot(high, clo_t[...])

    def cross(own, back):
        own_re, own_im = own[:, :PATCH], own[:, PATCH:]
        back_re, back_im = back[:, :PATCH], back[:, PATCH:]
        return [own_re * back_re + own_im * back_im, own_im * back_re - own_re * back_im]

    def surfaces_of(own, one, two):
        both = jnp.concatenate(cross(own, one) + cross(own, two), axis=1)
        high, low = halves(both)
        half = dot(high, lhi_t[...]) + dot(low, lhi_t[...]) + dot(high, llo_t[...])
        columns = [
            jnp.concatenate([half[n : n + HALF, :TILE], half[n : n + HALF, TILE:]], axis=0)
            for n in range(0, half.shape[0], HALF)
        ]
        high, low = halves(jnp.concatenate(columns, axis=1))
        wide = dot(up_t[...], jnp.concatenate([high, low, high], axis=0))
        joined = []
        for n in range(len(columns)):
            here = wide[:, n * TILE : (n + 1) * TILE]
            there = pltpu.roll(here, CROP, 1)
            both = here + there + here * there
            joined.append(jnp.where(left, both[: CROP // 2], both[CROP // 2 :]))
        return joined

    def spectrum(d, i):
        parts = row_transform(strip(d, i, 0, tiles))
        return col_transform([window(parts, j) for j in range(grid_cols)])

    def take_two(t, relayed):
        direct_two(t).wait_recv()
        if relayed:
            relay(t).start()
        if t == tiles:
            forward(2).start()

    for load in loads[:4]:
        load.wait()
    halo.wait_recv()
    for i in range(patch_rows):
        spec[0, i] = spectrum(0, i)
        early = order[:2] if i == 0 else order[2:-1]

        @pl.when(relays)
        def _(early=early):
            for t in early:
                take_two(t, True)

    @pl.when(jnp.logical_and(has_two, jnp.logical_not(relays)))
    def _():
        for t in order[:-1]:
            take_two(t, False)

    @pl.when(has_two)
    def _():
        forward(2).wait_recv()

    groups = [range(tiles - 1), range(tiles - 1, tiles)] if tiles > 1 else [range(tiles)]
    grown = {d: [[] for _ in range(patch_rows)] for d in (1, 2)}

    def windows_of(d, n):
        group = groups[n]
        final = n + 1 == len(groups)
        ready = range(
            2 * group[0] - 1 if n > 0 else 0, grid_cols if final else 2 * group[-1] + 1
        )
        slabs = [strip(d, i, group[0], len(group)) for i in range(patch_rows)]
        wide = row_transform(jnp.concatenate(slabs, axis=1))
        for i in range(patch_rows):
            grown[d][i] += wide[i * len(group) : (i + 1) * len(group)]
        return ready, [window(grown[d][i], j) for i in range(patch_rows) for j in ready]

    for n in range(len(groups)):
        if n + 1 == len(groups):

            @pl.when(relays)
            def _():
                take_two(order[-1], True)

            @pl.when(jnp.logical_and(has_two, jnp.logical_not(relays)))
            def _():
                take_two(order[-1], False)

            @pl.when(has_one)
            def _():
                direct_one(tiles).wait_recv()
                forward(1).start()

        ready, windows = windows_of(2, n)
        found = col_transform(windows)
        size = len(ready) * HALF
        for i in range(patch_rows):
            spec[1, i, pl.ds(ready[0] * HALF, size)] = found[i * size : (i + 1) * size]

    for load in loads[4:]:
        load.wait()

    rim_row = (patch_rows - 1) * other
    spans = []

    def send_rim(n):
        span = pl.ds(spans[n][0], len(spans[n]))
        return remote(
            agreed.at[rim_row, span], rim.at[span], rim_send.at[n], rim_recv.at[n], {"pln": other}
        )

    for n, group in enumerate(groups):

        @pl.when(has_one)
        def _(group=group, n=n):
            for t in group:
                direct_one(t).wait_recv()
            if n == 0:
                forward(1).wait_recv()

        ready, windows = windows_of(1, n)
        spans.append(ready)
        own, two = (
            jnp.concatenate(
                [spec[m, i, pl.ds(ready[0] * HALF, len(ready) * HALF)] for i in range(patch_rows)],
                axis=0,
            )
            for m in range(2)
        )
        joined = surfaces_of(own, col_transform(windows), two)
        for i in range(patch_rows):
            for m, j in enumerate(ready):
                agreed[i, j] = joined[i * len(ready) + m]
        send_rim(n).start()

    for n in range(len(groups)):
        send_rim(n).wait_recv()
    above = (p == 1).astype(jnp.float32)
    below = (p == 0).astype(jnp.float32)
    nothing = jnp.zeros((CROP // 2, TILE), jnp.float32)
    for i in range(patch_rows):
        stacked = [nothing]
        for j in range(grid_cols):
            up = agreed[i - 1, j] if i > 0 else rim[j] * above
            down = agreed[i + 1, j] if i < patch_rows - 1 else rim[j] * below
            stacked.append(up + 2.0 * agreed[i, j] + down)
        stacked.append(nothing)
        for j in range(grid_cols):
            o_ref[i, pl.ds(j, CROP // 2, stride=grid_cols), :] = (
                stacked[j] + 2.0 * stacked[j + 1] + stacked[j + 2]
            ) * (1.0 / 16.0)

    halo.wait_send()
    for n in range(len(groups)):
        send_rim(n).wait_send()
    for held, copy in ((gives_two, direct_two), (gives_one, direct_one), (relays, relay)):

        @pl.when(held)
        def _(copy=copy):
            for t in order:
                copy(t).wait_send()

    for d, here in ((1, has_one), (2, has_two)):

        @pl.when(here)
        def _(d=d):
            forward(d).wait_send()


def body(section_tiles):
    tile = section_tiles[0]
    rows, cols = tile.shape
    n_sec, n_pln = lax.axis_size("sec"), lax.axis_size("pln")
    assert n_pln == 2 and n_sec % 2 == 0 and cols % TILE == 0
    patch_rows, grid_cols, tiles = rows // STRIDE, cols // STRIDE, cols // TILE
    consts = tables()
    dma = pltpu.SemaphoreType.DMA
    out = pl.pallas_call(
        functools.partial(kernel, n_sec),
        out_shape=pltpu.VMEM((patch_rows, CROP // 2 * grid_cols, TILE), jnp.float32),
        in_specs=[pl.BlockSpec(memory_space=pl.ANY)] * (1 + len(consts)),
        out_specs=pl.BlockSpec(memory_space=pltpu.VMEM),
        scratch_shapes=[
            pltpu.VMEM((3, rows + 2 * MARGIN, cols), jnp.float32),
            *[pltpu.VMEM(const.shape, jnp.bfloat16) for const in consts],
            pltpu.VMEM((2, patch_rows, grid_cols * HALF, 2 * PATCH), jnp.float32),
            pltpu.VMEM((patch_rows, grid_cols, CROP // 2, TILE), jnp.float32),
            pltpu.VMEM((grid_cols, CROP // 2, TILE), jnp.float32),
            dma((1 + len(consts),)),
            dma((2,)),
            *[dma((tiles + 1,)) for _ in range(5)],
            *[dma((2,)) for _ in range(2)],
            *[dma((tiles,)) for _ in range(2)],
        ],
        compiler_params=pltpu.CompilerParams(
            collective_id=0, has_side_effects=True, vmem_limit_bytes=67043328 - 530 * 1024
        ),
    )(tile, *[jnp.asarray(const) for const in consts])
    out = out.reshape(patch_rows, CROP // 2, grid_cols, TILE)
    return out.transpose(0, 2, 1, 3).reshape(1, patch_rows, grid_cols, CROP * CROP)


def solution(mesh):
    placed = (P(("blocks", "sec"), "pln", None),)
    return jax.shard_map(
        body,
        mesh=mesh,
        in_specs=placed,
        out_specs=P(("blocks", "sec"), "pln", None, None),
        check_vma=False,
    )
```

```python
import functools
import math

import jax
import jax.numpy as jnp
import numpy as np
from jax import lax
from jax.experimental import pallas as pl
from jax.experimental.pallas import tpu as pltpu
from jax.sharding import PartitionSpec as P

PATCH = 128
STRIDE = 64
CROP = 64
MARGIN = 32
HALF = 72
TILE = 128
MESH = pl.DeviceIdType.MESH


def split_table(table):
    high = np.asarray(table, np.float32).astype(jnp.bfloat16)
    low = (np.asarray(table, np.float32) - high.astype(np.float32)).astype(jnp.bfloat16)
    return high, low


def angles(left, right):
    return np.mod(np.outer(left, right), PATCH) * (2.0 * math.pi / PATCH)


def tables():
    spots = np.arange(PATCH)
    freqs = np.arange(PATCH // 2 + 1)
    lags = np.arange(CROP) - CROP // 2
    rows = np.zeros((2 * HALF, PATCH))
    rows[: len(freqs)] = np.cos(angles(freqs, spots))
    rows[HALF : HALF + len(freqs)] = -np.sin(angles(freqs, spots))
    rows_hi, rows_lo = split_table(rows)
    row_table = np.concatenate([rows_hi, rows_hi, rows_lo], axis=1)
    cos, sin = np.cos(angles(spots, spots)), np.sin(angles(spots, spots))
    cols_hi, cols_lo = split_table(np.block([[cos, -sin], [sin, cos]]))
    cos, sin = np.cos(angles(spots, lags)), np.sin(angles(spots, lags))
    none = np.zeros_like(cos)
    lag_hi, lag_lo = split_table(
        np.block(
            [
                [cos, none, sin, none],
                [-sin, none, cos, none],
                [none, cos, none, sin],
                [none, -sin, none, cos],
            ]
        )
    )
    order = np.concatenate([lags[0::2], lags[1::2]])
    weight = np.where((freqs == 0) | (freqs == PATCH // 2), 1.0, 2.0) / PATCH**3
    ups = np.zeros((CROP, 2 * HALF))
    ups[:, : len(freqs)] = np.cos(angles(order, freqs)) * weight
    ups[:, HALF : HALF + len(freqs)] = -np.sin(angles(order, freqs)) * weight
    ups_hi, ups_lo = split_table(ups)
    up_table = np.concatenate([ups_hi, ups_hi, ups_lo], axis=1)
    return row_table, cols_hi, cols_lo, lag_hi, lag_lo, up_table


def halves(value):
    high = value.astype(jnp.bfloat16)
    return high, (value - high.astype(jnp.float32)).astype(jnp.bfloat16)


def dot(left, right):
    return jnp.dot(left, right, preferred_element_type=jnp.float32)


def kernel(
    n_sec, x_hbm, row_hbm, chi_hbm, clo_hbm, lhi_hbm, llo_hbm, up_hbm, o_ref,
    field, row_t, chi_t, clo_t, lhi_t, llo_t, up_t, spec, agreed, rim,
    load_sem, halo_sem, one_send, two_send, relay_send, one_recv, two_recv,
    fwd_send, fwd_recv, rim_send, rim_recv,
):
    rows, cols = x_hbm.shape
    tiles = cols // TILE
    patch_rows, grid_cols = rows // STRIDE, cols // STRIDE
    s, p = lax.axis_index("sec"), lax.axis_index("pln")
    other = 1 - p
    odd = lax.rem(s, 2) == 1
    has_one, has_two = s >= 1, s >= 2
    edge = pl.multiple_of(other * (rows - MARGIN), MARGIN)
    rest = pl.multiple_of(p * MARGIN, MARGIN)
    far = pl.multiple_of(p * (rows + MARGIN), MARGIN)

    loads = [
        pltpu.make_async_copy(src, dst, load_sem.at[n])
        for n, (src, dst) in enumerate(
            [
                (x_hbm, field.at[0, pl.ds(MARGIN, rows), :]),
                (row_hbm, row_t), (chi_hbm, chi_t), (clo_hbm, clo_t),
                (lhi_hbm, lhi_t), (llo_hbm, llo_t), (up_hbm, up_t),
            ]
        )
    ]
    for load in loads:
        load.start()

    barrier = pltpu.get_barrier_semaphore()
    count = jnp.int32(1)
    pl.semaphore_signal(barrier, inc=1, device_id={"pln": other}, device_id_type=MESH)
    for step in (-2, -1, 1, 2):
        there = jnp.logical_and(s + step >= 0, s + step < n_sec)
        count = count + there.astype(jnp.int32)

        @pl.when(there)
        def _(step=step):
            pl.semaphore_signal(barrier, inc=1, device_id={"sec": s + step}, device_id_type=MESH)

    pl.semaphore_wait(barrier, count)

    def remote(src, dst, send, recv, where):
        return pltpu.make_async_remote_copy(
            src_ref=src, dst_ref=dst, send_sem=send, recv_sem=recv,
            device_id=where, device_id_type=MESH,
        )

    def wrapped(step):
        return {"sec": lax.rem(s + step + n_sec, n_sec)}

    def piece(ref, t, shift):
        if t == tiles:
            return ref.at[pl.ds(pl.multiple_of(edge + shift, MARGIN), MARGIN), :]
        return ref.at[
            pl.ds(pl.multiple_of(rest + shift, MARGIN), rows - MARGIN), pl.ds(t * TILE, TILE)
        ]

    def landed(d, t):
        return piece(field.at[d], t, MARGIN)

    def direct_one(t):
        return remote(piece(x_hbm, t, 0), landed(1, t), one_send.at[t], one_recv.at[t], wrapped(1))

    def direct_two(t):
        return remote(piece(x_hbm, t, 0), landed(2, t), two_send.at[t], two_recv.at[t], wrapped(2))

    def relay(t):
        return remote(landed(2, t), landed(1, t), relay_send.at[t], one_recv.at[t], wrapped(-1))

    def forward(d):
        return remote(
            landed(d, tiles), field.at[d, pl.ds(far, MARGIN), :],
            fwd_send.at[d - 1], fwd_recv.at[d - 1], {"pln": other},
        )

    halo = remote(
        piece(x_hbm, tiles, 0), field.at[0, pl.ds(far, MARGIN), :],
        halo_sem.at[0], halo_sem.at[1], {"pln": other},
    )
    order = [tiles, *range(tiles)]
    gives_one = jnp.logical_and(jnp.logical_not(odd), s + 1 < n_sec)
    gives_two = s + 2 < n_sec
    relays = jnp.logical_and(odd, s >= 3)

    @pl.when(gives_two)
    def _():
        for t in order:
            direct_two(t).start()

    @pl.when(gives_one)
    def _():
        for t in order:
            direct_one(t).start()

    halo.start()

    for d in range(3):
        field[d, pl.ds(far, MARGIN), :] = jnp.zeros((MARGIN, cols), jnp.float32)
    for d, here in ((1, has_one), (2, has_two)):

        @pl.when(jnp.logical_not(here))
        def _(d=d):
            field[d] = jnp.zeros(field.shape[1:], jnp.float32)

    lane = lax.broadcasted_iota(jnp.int32, (2 * HALF, TILE), 1)
    left = lax.broadcasted_iota(jnp.int32, (CROP // 2, TILE), 1) < CROP
    zero = jnp.zeros((2 * HALF, TILE), jnp.float32)

    def strip(d, i, t, count):
        return field[d, pl.ds(i * STRIDE, PATCH), pl.ds(t * TILE, count * TILE)]

    def row_transform(slab):
        high, low = halves(slab)
        wide = dot(row_t[...], jnp.concatenate([high, low, high], axis=0))
        return [wide[:, n * TILE : (n + 1) * TILE] for n in range(slab.shape[1] // TILE)]

    def window(parts, j):
        t = j // 2
        if j % 2 == 0:
            before = parts[t - 1] if t > 0 else zero
            picked = jnp.where(lane < PATCH - MARGIN, parts[t], before)
        else:
            after = parts[t + 1] if t + 1 < tiles else zero
            picked = jnp.where(lane >= MARGIN, parts[t], after)
        return jnp.concatenate([picked[:HALF], picked[HALF:]], axis=1)

    def col_transform(windows):
        high, low = halves(jnp.concatenate(windows, axis=0))
        return dot(high, chi_t[...]) + dot(low, chi_t[...]) + dot(high, clo_t[...])

    def cross(own, back):
        own_re, own_im = own[:, :PATCH], own[:, PATCH:]
        back_re, back_im = back[:, :PATCH], back[:, PATCH:]
        return [own_re * back_re + own_im * back_im, own_im * back_re - own_re * back_im]

    def surfaces_of(own, one, two):
        both = jnp.concatenate(cross(own, one) + cross(own, two), axis=1)
        high, low = halves(both)
        half = dot(high, lhi_t[...]) + dot(low, lhi_t[...]) + dot(high, llo_t[...])
        columns = [
            jnp.concatenate([half[n : n + HALF, :TILE], half[n : n + HALF, TILE:]], axis=0)
            for n in range(0, half.shape[0], HALF)
        ]
        high, low = halves(jnp.concatenate(columns, axis=1))
        wide = dot(up_t[...], jnp.concatenate([high, low, high], axis=0))
        joined = []
        for n in range(len(columns)):
            here = wide[:, n * TILE : (n + 1) * TILE]
            there = pltpu.roll(here, CROP, 1)
            both = here + there + here * there
            joined.append(jnp.where(left, both[: CROP // 2], both[CROP // 2 :]))
        return joined

    def spectrum(d, i):
        parts = row_transform(strip(d, i, 0, tiles))
        return col_transform([window(parts, j) for j in range(grid_cols)])

    def take_two(t, relayed):
        direct_two(t).wait_recv()
        if relayed:
            relay(t).start()
        if t == tiles:
            forward(2).start()

    for load in loads[:4]:
        load.wait()
    halo.wait_recv()
    for i in range(patch_rows):
        spec[0, i] = spectrum(0, i)
        early = order[:2] if i == 0 else order[2:]

        @pl.when(relays)
        def _(early=early):
            for t in early:
                take_two(t, True)

    @pl.when(jnp.logical_and(has_two, jnp.logical_not(relays)))
    def _():
        for t in order[:-1]:
            take_two(t, False)

    @pl.when(has_two)
    def _():
        forward(2).wait_recv()

    groups = [range(tiles - 1), range(tiles - 1, tiles)] if tiles > 1 else [range(tiles)]
    grown = {d: [[] for _ in range(patch_rows)] for d in (1, 2)}

    def windows_of(d, n):
        group = groups[n]
        final = n + 1 == len(groups)
        ready = range(
            2 * group[0] - 1 if n > 0 else 0, grid_cols if final else 2 * group[-1] + 1
        )
        slabs = [strip(d, i, group[0], len(group)) for i in range(patch_rows)]
        wide = row_transform(jnp.concatenate(slabs, axis=1))
        for i in range(patch_rows):
            grown[d][i] += wide[i * len(group) : (i + 1) * len(group)]
        return ready, [window(grown[d][i], j) for i in range(patch_rows) for j in ready]

    for n in range(len(groups)):
        if n + 1 == len(groups):

            @pl.when(jnp.logical_and(has_two, jnp.logical_not(relays)))
            def _():
                take_two(order[-1], False)

            @pl.when(has_one)
            def _():
                direct_one(tiles).wait_recv()
                forward(1).start()

        ready, windows = windows_of(2, n)
        found = col_transform(windows)
        size = len(ready) * HALF
        for i in range(patch_rows):
            spec[1, i, pl.ds(ready[0] * HALF, size)] = found[i * size : (i + 1) * size]

    for load in loads[4:]:
        load.wait()

    rim_row = (patch_rows - 1) * other
    spans = []

    def send_rim(n):
        span = pl.ds(spans[n][0], len(spans[n]))
        return remote(
            agreed.at[rim_row, span], rim.at[span], rim_send.at[n], rim_recv.at[n], {"pln": other}
        )

    for n, group in enumerate(groups):

        @pl.when(has_one)
        def _(group=group, n=n):
            for t in group:
                direct_one(t).wait_recv()
            if n == 0:
                forward(1).wait_recv()

        ready, windows = windows_of(1, n)
        spans.append(ready)
        own, two = (
            jnp.concatenate(
                [spec[m, i, pl.ds(ready[0] * HALF, len(ready) * HALF)] for i in range(patch_rows)],
                axis=0,
            )
            for m in range(2)
        )
        joined = surfaces_of(own, col_transform(windows), two)
        for i in range(patch_rows):
            for m, j in enumerate(ready):
                agreed[i, j] = joined[i * len(ready) + m]
        send_rim(n).start()

    for n in range(len(groups)):
        send_rim(n).wait_recv()
    above = (p == 1).astype(jnp.float32)
    below = (p == 0).astype(jnp.float32)
    nothing = jnp.zeros((CROP // 2, TILE), jnp.float32)
    for i in range(patch_rows):
        stacked = [nothing]
        for j in range(grid_cols):
            up = agreed[i - 1, j] if i > 0 else rim[j] * above
            down = agreed[i + 1, j] if i < patch_rows - 1 else rim[j] * below
            stacked.append(up + 2.0 * agreed[i, j] + down)
        stacked.append(nothing)
        for j in range(grid_cols):
            o_ref[i, pl.ds(j, CROP // 2, stride=grid_cols), :] = (
                stacked[j] + 2.0 * stacked[j + 1] + stacked[j + 2]
            ) * (1.0 / 16.0)

    halo.wait_send()
    for n in range(len(groups)):
        send_rim(n).wait_send()
    for held, copy in ((gives_two, direct_two), (gives_one, direct_one), (relays, relay)):

        @pl.when(held)
        def _(copy=copy):
            for t in order:
                copy(t).wait_send()

    for d, here in ((1, has_one), (2, has_two)):

        @pl.when(here)
        def _(d=d):
            forward(d).wait_send()


def body(section_tiles):
    tile = section_tiles[0]
    rows, cols = tile.shape
    n_sec, n_pln = lax.axis_size("sec"), lax.axis_size("pln")
    assert n_pln == 2 and n_sec % 2 == 0 and cols % TILE == 0
    patch_rows, grid_cols, tiles = rows // STRIDE, cols // STRIDE, cols // TILE
    consts = tables()
    dma = pltpu.SemaphoreType.DMA
    out = pl.pallas_call(
        functools.partial(kernel, n_sec),
        out_shape=pltpu.VMEM((patch_rows, CROP // 2 * grid_cols, TILE), jnp.float32),
        in_specs=[pl.BlockSpec(memory_space=pl.ANY)] * (1 + len(consts)),
        out_specs=pl.BlockSpec(memory_space=pltpu.VMEM),
        scratch_shapes=[
            pltpu.VMEM((3, rows + 2 * MARGIN, cols), jnp.float32),
            *[pltpu.VMEM(const.shape, jnp.bfloat16) for const in consts],
            pltpu.VMEM((2, patch_rows, grid_cols * HALF, 2 * PATCH), jnp.float32),
            pltpu.VMEM((patch_rows, grid_cols, CROP // 2, TILE), jnp.float32),
            pltpu.VMEM((grid_cols, CROP // 2, TILE), jnp.float32),
            dma((1 + len(consts),)),
            dma((2,)),
            *[dma((tiles + 1,)) for _ in range(5)],
            *[dma((2,)) for _ in range(2)],
            *[dma((tiles,)) for _ in range(2)],
        ],
        compiler_params=pltpu.CompilerParams(
            collective_id=0, has_side_effects=True, vmem_limit_bytes=67043328 - 530 * 1024
        ),
    )(tile, *[jnp.asarray(const) for const in consts])
    out = out.reshape(patch_rows, CROP // 2, grid_cols, TILE)
    return out.transpose(0, 2, 1, 3).reshape(1, patch_rows, grid_cols, CROP * CROP)


def solution(mesh):
    placed = (P(("blocks", "sec"), "pln", None),)
    return jax.shard_map(
        body,
        mesh=mesh,
        in_specs=placed,
        out_specs=P(("blocks", "sec"), "pln", None, None),
        check_vma=False,
    )
```

```python
import functools
import math

import jax
import jax.numpy as jnp
import numpy as np
from jax import lax
from jax.experimental import pallas as pl
from jax.experimental.pallas import tpu as pltpu
from jax.sharding import PartitionSpec as P

PATCH = 128
STRIDE = 64
CROP = 64
MARGIN = 32
HALF = 72
TILE = 128
MESH = pl.DeviceIdType.MESH


def split_table(table):
    high = np.asarray(table, np.float32).astype(jnp.bfloat16)
    low = (np.asarray(table, np.float32) - high.astype(np.float32)).astype(jnp.bfloat16)
    return high, low


def angles(left, right):
    return np.mod(np.outer(left, right), PATCH) * (2.0 * math.pi / PATCH)


def tables():
    spots = np.arange(PATCH)
    freqs = np.arange(PATCH // 2 + 1)
    lags = np.arange(CROP) - CROP // 2
    rows = np.zeros((2 * HALF, PATCH))
    rows[: len(freqs)] = np.cos(angles(freqs, spots))
    rows[HALF : HALF + len(freqs)] = -np.sin(angles(freqs, spots))
    rows_hi, rows_lo = split_table(rows)
    row_table = np.concatenate([rows_hi, rows_hi, rows_lo], axis=1)
    cos, sin = np.cos(angles(spots, spots)), np.sin(angles(spots, spots))
    cols_hi, cols_lo = split_table(np.block([[cos, -sin], [sin, cos]]))
    cos, sin = np.cos(angles(spots, lags)), np.sin(angles(spots, lags))
    none = np.zeros_like(cos)
    lag_hi, lag_lo = split_table(
        np.block(
            [
                [cos, none, sin, none],
                [-sin, none, cos, none],
                [none, cos, none, sin],
                [none, -sin, none, cos],
            ]
        )
    )
    order = np.concatenate([lags[0::2], lags[1::2]])
    weight = np.where((freqs == 0) | (freqs == PATCH // 2), 1.0, 2.0) / PATCH**3
    ups = np.zeros((CROP, 2 * HALF))
    ups[:, : len(freqs)] = np.cos(angles(order, freqs)) * weight
    ups[:, HALF : HALF + len(freqs)] = -np.sin(angles(order, freqs)) * weight
    ups_hi, ups_lo = split_table(ups)
    up_table = np.concatenate([ups_hi, ups_hi, ups_lo], axis=1)
    return row_table, cols_hi, cols_lo, lag_hi, lag_lo, up_table


def halves(value):
    high = value.astype(jnp.bfloat16)
    return high, (value - high.astype(jnp.float32)).astype(jnp.bfloat16)


def dot(left, right):
    return jnp.dot(left, right, preferred_element_type=jnp.float32)


def kernel(
    n_sec, x_hbm, row_hbm, chi_hbm, clo_hbm, lhi_hbm, llo_hbm, up_hbm, o_ref,
    field, row_t, chi_t, clo_t, lhi_t, llo_t, up_t, spec, agreed, rim,
    load_sem, halo_sem, one_send, two_send, relay_send, one_recv, two_recv,
    fwd_send, fwd_recv, rim_send, rim_recv,
):
    rows, cols = x_hbm.shape
    tiles = cols // TILE
    patch_rows, grid_cols = rows // STRIDE, cols // STRIDE
    s, p = lax.axis_index("sec"), lax.axis_index("pln")
    other = 1 - p
    odd = lax.rem(s, 2) == 1
    has_one, has_two = s >= 1, s >= 2
    edge = pl.multiple_of(other * (rows - MARGIN), MARGIN)
    rest = pl.multiple_of(p * MARGIN, MARGIN)
    far = pl.multiple_of(p * (rows + MARGIN), MARGIN)

    loads = [
        pltpu.make_async_copy(src, dst, load_sem.at[n])
        for n, (src, dst) in enumerate(
            [
                (x_hbm, field.at[0, pl.ds(MARGIN, rows), :]),
                (row_hbm, row_t), (chi_hbm, chi_t), (clo_hbm, clo_t),
                (lhi_hbm, lhi_t), (llo_hbm, llo_t), (up_hbm, up_t),
            ]
        )
    ]
    for load in loads:
        load.start()

    barrier = pltpu.get_barrier_semaphore()
    count = jnp.int32(1)
    pl.semaphore_signal(barrier, inc=1, device_id={"pln": other}, device_id_type=MESH)
    for step in (-2, -1, 1, 2):
        there = jnp.logical_and(s + step >= 0, s + step < n_sec)
        count = count + there.astype(jnp.int32)

        @pl.when(there)
        def _(step=step):
            pl.semaphore_signal(barrier, inc=1, device_id={"sec": s + step}, device_id_type=MESH)

    pl.semaphore_wait(barrier, count)

    def remote(src, dst, send, recv, where):
        return pltpu.make_async_remote_copy(
            src_ref=src, dst_ref=dst, send_sem=send, recv_sem=recv,
            device_id=where, device_id_type=MESH,
        )

    def wrapped(step):
        return {"sec": lax.rem(s + step + n_sec, n_sec)}

    def piece(ref, t, shift):
        if t == tiles:
            return ref.at[pl.ds(pl.multiple_of(edge + shift, MARGIN), MARGIN), :]
        return ref.at[
            pl.ds(pl.multiple_of(rest + shift, MARGIN), rows - MARGIN), pl.ds(t * TILE, TILE)
        ]

    def landed(d, t):
        return piece(field.at[d], t, MARGIN)

    def direct_one(t):
        return remote(piece(x_hbm, t, 0), landed(1, t), one_send.at[t], one_recv.at[t], wrapped(1))

    def direct_two(t):
        return remote(piece(x_hbm, t, 0), landed(2, t), two_send.at[t], two_recv.at[t], wrapped(2))

    def relay(t):
        return remote(landed(2, t), landed(1, t), relay_send.at[t], one_recv.at[t], wrapped(-1))

    def forward(d):
        return remote(
            landed(d, tiles), field.at[d, pl.ds(far, MARGIN), :],
            fwd_send.at[d - 1], fwd_recv.at[d - 1], {"pln": other},
        )

    halo = remote(
        piece(x_hbm, tiles, 0), field.at[0, pl.ds(far, MARGIN), :],
        halo_sem.at[0], halo_sem.at[1], {"pln": other},
    )
    order = [tiles, *range(tiles)]
    gives_one = jnp.logical_and(jnp.logical_not(odd), s + 1 < n_sec)
    gives_two = s + 2 < n_sec
    relays = jnp.logical_and(odd, s >= 3)

    @pl.when(gives_two)
    def _():
        for t in order:
            direct_two(t).start()

    @pl.when(gives_one)
    def _():
        for t in order:
            direct_one(t).start()

    halo.start()

    for d in range(3):
        field[d, pl.ds(far, MARGIN), :] = jnp.zeros((MARGIN, cols), jnp.float32)
    for d, here in ((1, has_one), (2, has_two)):

        @pl.when(jnp.logical_not(here))
        def _(d=d):
            field[d] = jnp.zeros(field.shape[1:], jnp.float32)

    lane = lax.broadcasted_iota(jnp.int32, (2 * HALF, TILE), 1)
    left = lax.broadcasted_iota(jnp.int32, (CROP // 2, TILE), 1) < CROP
    zero = jnp.zeros((2 * HALF, TILE), jnp.float32)

    def strip(d, i, t, count):
        return field[d, pl.ds(i * STRIDE, PATCH), pl.ds(t * TILE, count * TILE)]

    def row_transform(slab):
        high, low = halves(slab)
        wide = dot(row_t[...], jnp.concatenate([high, low, high], axis=0))
        return [wide[:, n * TILE : (n + 1) * TILE] for n in range(slab.shape[1] // TILE)]

    def window(parts, j):
        t = j // 2
        if j % 2 == 0:
            before = parts[t - 1] if t > 0 else zero
            picked = jnp.where(lane < PATCH - MARGIN, parts[t], before)
        else:
            after = parts[t + 1] if t + 1 < tiles else zero
            picked = jnp.where(lane >= MARGIN, parts[t], after)
        return jnp.concatenate([picked[:HALF], picked[HALF:]], axis=1)

    def col_transform(windows):
        high, low = halves(jnp.concatenate(windows, axis=0))
        return dot(high, chi_t[...]) + dot(low, chi_t[...]) + dot(high, clo_t[...])

    def cross(own, back):
        own_re, own_im = own[:, :PATCH], own[:, PATCH:]
        back_re, back_im = back[:, :PATCH], back[:, PATCH:]
        return [own_re * back_re + own_im * back_im, own_im * back_re - own_re * back_im]

    def surfaces_of(own, one, two):
        both = jnp.concatenate(cross(own, one) + cross(own, two), axis=1)
        high, low = halves(both)
        half = dot(high, lhi_t[...]) + dot(low, lhi_t[...]) + dot(high, llo_t[...])
        columns = [
            jnp.concatenate([half[n : n + HALF, :TILE], half[n : n + HALF, TILE:]], axis=0)
            for n in range(0, half.shape[0], HALF)
        ]
        high, low = halves(jnp.concatenate(columns, axis=1))
        wide = dot(up_t[...], jnp.concatenate([high, low, high], axis=0))
        joined = []
        for n in range(len(columns)):
            here = wide[:, n * TILE : (n + 1) * TILE]
            there = pltpu.roll(here, CROP, 1)
            both = here + there + here * there
            joined.append(jnp.where(left, both[: CROP // 2], both[CROP // 2 :]))
        return joined

    def spectrum(d, i):
        parts = row_transform(strip(d, i, 0, tiles))
        return col_transform([window(parts, j) for j in range(grid_cols)])

    def take_two(t, relayed):
        direct_two(t).wait_recv()
        if relayed:
            relay(t).start()
        if t == tiles:
            forward(2).start()

    for load in loads[:4]:
        load.wait()
    halo.wait_recv()
    for i in range(patch_rows + 1):
        early = order[2 * i : 2 * i + 2] if i < patch_rows else order[2 * i :]

        @pl.when(relays)
        def _(early=early):
            for t in early:
                take_two(t, True)

        if i < patch_rows:
            spec[0, i] = spectrum(0, i)

    @pl.when(jnp.logical_and(has_two, jnp.logical_not(relays)))
    def _():
        for t in order[:-1]:
            take_two(t, False)

    @pl.when(has_two)
    def _():
        forward(2).wait_recv()

    groups = [range(tiles - 1), range(tiles - 1, tiles)] if tiles > 1 else [range(tiles)]
    grown = {d: [[] for _ in range(patch_rows)] for d in (1, 2)}

    def windows_of(d, n):
        group = groups[n]
        final = n + 1 == len(groups)
        ready = range(
            2 * group[0] - 1 if n > 0 else 0, grid_cols if final else 2 * group[-1] + 1
        )
        slabs = [strip(d, i, group[0], len(group)) for i in range(patch_rows)]
        wide = row_transform(jnp.concatenate(slabs, axis=1))
        for i in range(patch_rows):
            grown[d][i] += wide[i * len(group) : (i + 1) * len(group)]
        return ready, [window(grown[d][i], j) for i in range(patch_rows) for j in ready]

    for n in range(len(groups)):
        if n + 1 == len(groups):

            @pl.when(jnp.logical_and(has_two, jnp.logical_not(relays)))
            def _():
                take_two(order[-1], False)

            @pl.when(has_one)
            def _():
                direct_one(tiles).wait_recv()
                forward(1).start()

        ready, windows = windows_of(2, n)
        found = col_transform(windows)
        size = len(ready) * HALF
        for i in range(patch_rows):
            spec[1, i, pl.ds(ready[0] * HALF, size)] = found[i * size : (i + 1) * size]

    for load in loads[4:]:
        load.wait()

    rim_row = (patch_rows - 1) * other
    spans = []

    def send_rim(n):
        span = pl.ds(spans[n][0], len(spans[n]))
        return remote(
            agreed.at[rim_row, span], rim.at[span], rim_send.at[n], rim_recv.at[n], {"pln": other}
        )

    for n, group in enumerate(groups):

        @pl.when(has_one)
        def _(group=group, n=n):
            for t in group:
                direct_one(t).wait_recv()
            if n == 0:
                forward(1).wait_recv()

        ready, windows = windows_of(1, n)
        spans.append(ready)
        own, two = (
            jnp.concatenate(
                [spec[m, i, pl.ds(ready[0] * HALF, len(ready) * HALF)] for i in range(patch_rows)],
                axis=0,
            )
            for m in range(2)
        )
        joined = surfaces_of(own, col_transform(windows), two)
        for i in range(patch_rows):
            for m, j in enumerate(ready):
                agreed[i, j] = joined[i * len(ready) + m]
        send_rim(n).start()

    for n in range(len(groups)):
        send_rim(n).wait_recv()
    above = (p == 1).astype(jnp.float32)
    below = (p == 0).astype(jnp.float32)
    nothing = jnp.zeros((CROP // 2, TILE), jnp.float32)
    for i in range(patch_rows):
        stacked = [nothing]
        for j in range(grid_cols):
            up = agreed[i - 1, j] if i > 0 else rim[j] * above
            down = agreed[i + 1, j] if i < patch_rows - 1 else rim[j] * below
            stacked.append(up + 2.0 * agreed[i, j] + down)
        stacked.append(nothing)
        for j in range(grid_cols):
            o_ref[i, pl.ds(j, CROP // 2, stride=grid_cols), :] = (
                stacked[j] + 2.0 * stacked[j + 1] + stacked[j + 2]
            ) * (1.0 / 16.0)

    halo.wait_send()
    for n in range(len(groups)):
        send_rim(n).wait_send()
    for held, copy in ((gives_two, direct_two), (gives_one, direct_one), (relays, relay)):

        @pl.when(held)
        def _(copy=copy):
            for t in order:
                copy(t).wait_send()

    for d, here in ((1, has_one), (2, has_two)):

        @pl.when(here)
        def _(d=d):
            forward(d).wait_send()


def body(section_tiles):
    tile = section_tiles[0]
    rows, cols = tile.shape
    n_sec, n_pln = lax.axis_size("sec"), lax.axis_size("pln")
    assert n_pln == 2 and n_sec % 2 == 0 and cols % TILE == 0
    patch_rows, grid_cols, tiles = rows // STRIDE, cols // STRIDE, cols // TILE
    consts = tables()
    dma = pltpu.SemaphoreType.DMA
    out = pl.pallas_call(
        functools.partial(kernel, n_sec),
        out_shape=pltpu.VMEM((patch_rows, CROP // 2 * grid_cols, TILE), jnp.float32),
        in_specs=[pl.BlockSpec(memory_space=pl.ANY)] * (1 + len(consts)),
        out_specs=pl.BlockSpec(memory_space=pltpu.VMEM),
        scratch_shapes=[
            pltpu.VMEM((3, rows + 2 * MARGIN, cols), jnp.float32),
            *[pltpu.VMEM(const.shape, jnp.bfloat16) for const in consts],
            pltpu.VMEM((2, patch_rows, grid_cols * HALF, 2 * PATCH), jnp.float32),
            pltpu.VMEM((patch_rows, grid_cols, CROP // 2, TILE), jnp.float32),
            pltpu.VMEM((grid_cols, CROP // 2, TILE), jnp.float32),
            dma((1 + len(consts),)),
            dma((2,)),
            *[dma((tiles + 1,)) for _ in range(5)],
            *[dma((2,)) for _ in range(2)],
            *[dma((tiles,)) for _ in range(2)],
        ],
        compiler_params=pltpu.CompilerParams(
            collective_id=0, has_side_effects=True, vmem_limit_bytes=67043328 - 530 * 1024
        ),
    )(tile, *[jnp.asarray(const) for const in consts])
    out = out.reshape(patch_rows, CROP // 2, grid_cols, TILE)
    return out.transpose(0, 2, 1, 3).reshape(1, patch_rows, grid_cols, CROP * CROP)


def solution(mesh):
    placed = (P(("blocks", "sec"), "pln", None),)
    return jax.shard_map(
        body,
        mesh=mesh,
        in_specs=placed,
        out_specs=P(("blocks", "sec"), "pln", None, None),
        check_vma=False,
    )
```
